512 devices in a mesh: dp: 8 (over z_lo, core), expert: 64 (over x, z_hi, y).
Axes of the slice: x: 4, y: 4, z: 16 (z_hi: 4, z_lo: 4; z = z_hi * 4 + z_lo), core: 2. Of those that a mesh axis runs over, the one named last changes fastest.
Arguments:
- tokens: bfloat16 [32768, 2560], P(('dp', 'expert')), may hold values from -6 to 6
- cotangent: bfloat16 [32768, 2560], P(('dp', 'expert')), may hold values from -0.59765625 to 0.59765625
- w_gate: bfloat16 [64, 2560, 768], P('expert', 'dp'), may hold values from -0.125 to 0.125
- w_up: bfloat16 [64, 2560, 768], P('expert', 'dp'), may hold values from -0.125 to 0.125
- expert_ids: int32 [32768, 6], P(('dp', 'expert')), may hold values from 0 to 63, all different within a row; in each aligned block of 64 rows (0 to 63, 64 to 127, ...) at most 7 rows name the same one
- gate_num: int32 [32768, 6], P(('dp', 'expert')), may hold values from 1 to 64
- swap_flags: int32 [32], replicated, may hold values 0 or 1
Outputs:
- grad_held: float32 [64, 768, 2560], P('expert', 'dp')
The draws below stay inside these ranges and needn't reach their ends.
Inputs may be any that keep to these rules, and one draw needn't show every extreme that they name: `expert_ids`: each row names 6 different experts; the 64 rows of one device name no expert more than 7 times, a bound that some block reaches.
All inputs are finite; a program needn't handle non-finite values.
Results may differ from the reference program's by a relative error of at most 0.015.
Values may be sent and summed in bfloat16 or wider, within the bound.
No kernel may reach another device: no remote copies, remote signals or barrier semaphores. Data moves between devices by JAX's collectives and lax.ppermute only.
A program may use at most 64 MiB of HBM per device.

```python
import math
import jax
import jax.numpy as jnp
import numpy as np
from jax import lax

D = 2560
FF = 768
TOPK = 6
TOK_DEV = 64
EXPERTS = 64
CAP = 7
TOKENS = 32768
N_DP = 8
N_EXPERT = 64


def plant(array, rng, least, high):
    longest = array.shape.index(max(array.shape))
    spots = []
    for shift in (0, 1):
        where = [jax.random.randint(jax.random.fold_in(rng, axis), (), 0, length) for axis, length in enumerate(array.shape)]
        where[longest] = (where[longest] + shift) % array.shape[longest]
        spots.append(tuple(where))
    return array.at[spots[0]].set(least).at[spots[1]].set(high)


def level_of(stream_key, dims, cuts, low, top_value):
    def one(dim, shards_of):
        draws = jax.random.uniform(jax.random.fold_in(jax.random.fold_in(stream_key, 6), dim), (shards_of,), jnp.float32, low / len(cuts), top_value / len(cuts))
        return jnp.repeat(jnp.exp(draws), dims[dim] // shards_of).reshape((-1,) + (1,) * (len(dims) - dim - 1))

    factor_of = one(*cuts[0])
    for cut in cuts[1:]:
        factor_of = factor_of * one(*cut)
    return factor_of


def assign_block(key, own, number, rows, number_of, top, most, skew):
    order = jax.random.permutation(key, number_of)
    crowded, ordinary = load_shares(number_of, rows * top, most, skew, True), load_shares(number_of, rows * top, most, skew, False)
    places = jnp.arange(number_of)

    def named(lengths, rotation):
        used = int((lengths > 0).sum())
        fixed = max(1, used // 4)
        shifted = fixed + (places - fixed + rotation * (used - fixed)) % max(1, number_of - fixed)
        return jnp.zeros((number_of,), jnp.int32).at[order[jnp.where(places < fixed, places, shifted)]].set(jnp.asarray(lengths, jnp.int32))

    lengths = jnp.where(number % 4 == 0, named(crowded, number // 4), named(ordinary, number - number // 4 - 1))
    mixed = jax.random.permutation(jax.random.fold_in(own, 3), number_of)
    donor, sink = mixed[0:number_of // 2 * 2:2], mixed[1:number_of // 2 * 2:2]
    room = jnp.minimum(lengths[donor] - 1, most - lengths[sink]) // 2
    room = jnp.where((donor == order[0]) | (sink == order[0]) | (lengths[sink] == 0), 0, jnp.maximum(room, 0))
    shifted = jax.random.randint(jax.random.fold_in(own, 4), (number_of // 2,), 0, 1 << 20) % (room + 1)
    lengths = lengths.at[donor].add(-shifted).at[sink].add(shifted)
    items = jnp.searchsorted(jnp.cumsum(lengths), jnp.arange(rows * top), side="right").astype(jnp.int32)
    grid = items.reshape(top, rows).T
    grid = grid[jax.random.permutation(jax.random.fold_in(own, 1), rows)]
    rotation = jax.random.randint(jax.random.fold_in(own, 2), (rows, 1), 0, top)
    return jnp.take_along_axis(grid, (jnp.arange(top)[None, :] + rotation) % top, axis=1)


def load_shares(number_of, total, most, lean, full):
    portions = [(1 << 20) // math.isqrt(standing ** lean) + 1 for standing in range(1, number_of + 1)]
    largest = most if full else min(most, max(-(-total // number_of), total * portions[0] // sum(portions)))
    least = 1 if total - largest >= number_of - 1 else 0
    counts, surplus = [largest] + [least] * (number_of - 1), total - largest - least * (number_of - 1)
    while surplus > 0:
        movable = [i for i in range(1, number_of) if counts[i] < largest] or [i for i in range(1, number_of) if counts[i] < most]
        pool, budget = sum([portions[i] for i in movable]), surplus
        for i in movable:
            addition = min(most - counts[i], max(1, budget * portions[i] // pool), surplus)
            counts[i] = counts[i] + addition
            surplus = surplus - addition
    return np.array(counts)


def normal_values(rng, extent, deviation, bound, pieces=(), kind=jnp.bfloat16):
    loudness = level_of(rng, extent, pieces, -0.22, 0.18) if pieces else 1.0
    array = jax.random.normal(rng, extent, jnp.float32) * deviation * loudness
    return jnp.minimum(jnp.maximum(array, -bound), bound).astype(kind)


def setup_inputs(seed: int = 0) -> dict:
    key_of = jax.random.split(jax.random.key(seed), 8)
    tokens = normal_values(key_of[0], (TOKENS, D), 1.0, 6.0, ((0, 512),))
    cotangent = normal_values(key_of[1], (TOKENS, D), 0.1, 0.59765625, ((0, 512),))
    w_gate = normal_values(key_of[2], (EXPERTS, D, FF), D ** -0.5, 0.125, ((0, 64), (1, 8)))
    w_up = normal_values(key_of[3], (EXPERTS, D, FF), D ** -0.5, 0.125, ((0, 64), (1, 8)))
    expert_ids_keys = jax.random.split(jax.random.fold_in(key_of[4], 1), TOKENS // TOK_DEV)
    expert_ids_turns = jax.random.permutation(jax.random.fold_in(key_of[4], 3), TOKENS // TOK_DEV)
    expert_ids = jax.vmap(lambda own, number: assign_block(jax.random.fold_in(key_of[4], 2), own, number, TOK_DEV, EXPERTS, TOPK, CAP, 2))(expert_ids_keys, expert_ids_turns).reshape((TOKENS, TOPK))
    gate_num = plant(jax.random.randint(key_of[5], (TOKENS, TOPK), 1, 65), jax.random.fold_in(key_of[5], 1), 1, 64).astype(jnp.int32)
    swap_flags = plant((jax.random.randint(key_of[6], (EXPERTS // 2,), 0, 2) < 1).astype(jnp.int32), jax.random.fold_in(key_of[6], 1), 0, 1)
    return dict(tokens=tokens, cotangent=cotangent, w_gate=w_gate, w_up=w_up, expert_ids=expert_ids, gate_num=gate_num, swap_flags=swap_flags)


def expert_terms(x_rows, dy_rows, ids_rows, num_rows, w_gate, w_up):
    assigned = ids_rows.reshape(-1).astype(jnp.int32)
    total = assigned.shape[0]
    one_hot = (assigned[:, None] == jnp.arange(EXPERTS, dtype=jnp.int32)[None, :]).astype(jnp.int32)
    ranking = jnp.sum((jnp.cumsum(one_hot, axis=0) - one_hot) * one_hot, axis=1).astype(jnp.int32)
    slot_count = N_EXPERT * CAP
    table = jnp.full((EXPERTS, slot_count), total, jnp.int32)
    table = table.at[assigned, ranking].set(jnp.arange(total, dtype=jnp.int32))
    usable = table < total
    clipped = jnp.minimum(table, total - 1).astype(jnp.int32)
    token_index = (clipped // TOPK).astype(jnp.int32)
    numbers = num_rows.reshape(-1)[clipped].astype(jnp.float32)
    weights = jnp.where(usable, numbers / 64.0, jnp.float32(0.0)).astype(jnp.float32)

    def one_expert(inputs):
        index_row, weight_row, gate_matrix, up_matrix = inputs
        chosen = x_rows[index_row]
        gate = jnp.dot(chosen, gate_matrix, preferred_element_type=jnp.float32)
        upper = jnp.dot(chosen, up_matrix, preferred_element_type=jnp.float32)
        hidden = (jax.nn.silu(gate) * upper).astype(jnp.bfloat16)
        scaled = (weight_row[:, None] * dy_rows[index_row].astype(jnp.float32)).astype(jnp.bfloat16)
        term = lax.dot_general(hidden, scaled, (((0,), (0,)), ((), ())), preferred_element_type=jnp.float32)
        term = lax.optimization_barrier(term.astype(jnp.bfloat16))
        return term.astype(jnp.float32)

    return lax.map(one_expert, (token_index, weights, w_gate, w_up))


def reference(tokens, cotangent, w_gate, w_up, expert_ids, gate_num, swap_flags):
    group_rows = TOK_DEV * N_EXPERT

    def add_group(index, accumulated):
        start = (index * group_rows).astype(jnp.int32)
        x_rows = lax.dynamic_slice_in_dim(tokens, start, group_rows, 0)
        dy_rows = lax.dynamic_slice_in_dim(cotangent, start, group_rows, 0)
        ids_rows = lax.dynamic_slice_in_dim(expert_ids, start, group_rows, 0)
        num_rows = lax.dynamic_slice_in_dim(gate_num, start, group_rows, 0)
        return accumulated + expert_terms(x_rows, dy_rows, ids_rows, num_rows, w_gate, w_up)

    accumulated = lax.fori_loop(0, N_DP, add_group, jnp.zeros((EXPERTS, FF, D), jnp.float32))
    half_count = EXPERTS // 2
    experts = jnp.arange(EXPERTS, dtype=jnp.int32)
    held = jnp.where(swap_flags[experts % half_count] == 1, (experts + half_count) % EXPERTS, experts).astype(jnp.int32)
    return accumulated[held]
```

```python
import functools

import jax
import jax.numpy as jnp
from jax import lax
from jax.experimental import pallas as pl
from jax.experimental.pallas import tpu as pltpu
from jax.sharding import Mesh, PartitionSpec as P

PLANE = ("x", "y")
RANKS = 8


def route_kernel(count, weighted, scale_ref, flags_ref, place_ref, *refs):
    metas, rows, out_ref, pick_ref = refs[:count], refs[count : 2 * count], refs[2 * count], refs[2 * count + 1]
    tok_count = metas[0].shape[0]
    slots = pick_ref.shape[2]

    @pl.when(pl.program_id(0) == 0)
    def _():
        lane = lax.broadcasted_iota(jnp.int32, (1, slots), 1)
        expert = jnp.zeros((1, slots), jnp.int32)
        for j in range(16):
            home = (j // 4) * 16 + place_ref[0] * 4 + j % 4
            other = lax.rem(home + 32, 64)
            held = jnp.where(flags_ref[lax.rem(home, 32)] == 1, other, home)
            expert = jnp.where(lane // RANKS == j, held, expert)
        expert = expert.astype(jnp.float32)
        rank_of = (lane % RANKS).astype(jnp.float32)
        earlier = (
            lax.broadcasted_iota(jnp.int32, (tok_count, tok_count), 0)
            > lax.broadcasted_iota(jnp.int32, (tok_count, tok_count), 1)
        ).astype(jnp.bfloat16)
        for s in range(count):
            meta = metas[s][...].astype(jnp.float32)
            chosen = jnp.zeros((tok_count, slots), jnp.float32)
            weight = jnp.zeros((tok_count, slots), jnp.float32)
            for k in range(6):
                hit = meta[:, k : k + 1] == expert
                chosen = jnp.where(hit, 1.0, chosen)
                if weighted:
                    weight = jnp.where(hit, meta[:, 6 + k : 7 + k] * scale_ref[0], weight)
            before = jnp.dot(earlier, chosen.astype(jnp.bfloat16), preferred_element_type=jnp.float32)
            value = weight if weighted else chosen
            pick_ref[s] = jnp.where((before == rank_of) & (chosen > 0.0), value, 0.0).astype(jnp.bfloat16)

    for s in range(count):
        picked = lax.dot_general(
            pick_ref[s], rows[s][...], (((0,), (0,)), ((), ())), preferred_element_type=jnp.float32
        )
        width = picked.shape[1]
        out_ref[:, s * RANKS : (s + 1) * RANKS, :] = picked.reshape(16, RANKS, width).astype(jnp.bfloat16)


def route(flags, place, metas, rows, width, weighted):
    count = len(rows)
    tok_count = rows[0].shape[0]
    tile = 512
    meta_block = width // 128
    smem = pl.BlockSpec(memory_space=pltpu.SMEM)
    scale = jnp.full((1,), 1.0 / 64.0, jnp.float32)
    return pl.pallas_call(
        functools.partial(route_kernel, count, weighted),
        grid=(width // tile,),
        in_specs=[smem] * 3
        + [pl.BlockSpec((tok_count, 128), lambda i: (0, meta_block))] * count
        + [pl.BlockSpec((tok_count, tile), lambda i: (0, i))] * count,
        out_specs=pl.BlockSpec((16, count * RANKS, tile), lambda i: (0, 0, i)),
        out_shape=jax.ShapeDtypeStruct((16, count * RANKS, width), jnp.bfloat16),
        scratch_shapes=[pltpu.VMEM((count, tok_count, 16 * RANKS), jnp.bfloat16)],
        cost_estimate=pl.CostEstimate(
            flops=2 * count * tok_count * 128 * width,
            bytes_accessed=count * (tok_count + 128) * width * 2,
            transcendentals=0,
        ),
    )(scale, flags, place, *metas, *rows)


def plane_exchange(value):
    got = lax.all_to_all(value, PLANE, split_axis=0, concat_axis=0, tiled=True)
    return got.reshape(-1, value.shape[2])


def shards(tokens, cotangent, w_gate, w_up, expert_ids, gate_num, swap_flags):
    width = tokens.shape[1]
    up, down = [(i, (i + 1) % 4) for i in range(4)], [(i, (i - 1) % 4) for i in range(4)]
    opposite = [(i, (i + 2) % 4) for i in range(4)]
    place = lax.axis_index("zh")
    me = (lax.axis_index("x") * 4 + place) * 4 + lax.axis_index("y")
    place = place.reshape(1)
    meta = jnp.concatenate([expert_ids, gate_num], axis=1).astype(jnp.bfloat16)
    meta = jnp.pad(meta, ((0, 0), (0, 128 - meta.shape[1])))
    tok = jnp.concatenate([tokens, meta], axis=1)
    tok_l = lax.ppermute(tok, "zh", up)
    tok_r = lax.ppermute(tok, "zh", down)
    cot_l = lax.ppermute(cotangent, "zh", up)
    cot_r = lax.ppermute(cotangent, "zh", down)
    tok_o = lax.ppermute(tok_l, "zh", up)
    cot_o = lax.ppermute(cot_r, "zh", down)
    my_flag = swap_flags[me % 32] == 1
    weights = jnp.concatenate([w_gate[0], w_up[0]], axis=1)
    other = lax.ppermute(weights, "x", opposite)
    weights = jnp.where(my_flag, other, weights)
    full = lax.all_gather(weights, ("zl", "c"), axis=0, tiled=True)
    send = functools.partial(route, swap_flags, place, width=width)
    near = [tok, tok_l, tok_r]
    x_near = plane_exchange(send(near, near, weighted=False))
    y_near = plane_exchange(send(near, [cotangent, cot_l, cot_r], weighted=True))
    x_far = plane_exchange(send([tok_o], [tok_o], weighted=False))
    y_far = plane_exchange(send([tok_o], [cot_o], weighted=True))

    def hidden_of(rows):
        both = jnp.dot(rows, full, preferred_element_type=jnp.float32)
        gate, upper = both[:, :768], both[:, 768:]
        return (jax.nn.silu(gate) * upper).astype(jnp.bfloat16)

    hidden = jnp.concatenate([hidden_of(x_near), hidden_of(x_far)], axis=0)
    scaled = jnp.concatenate([y_near, y_far], axis=0)
    grads = lax.psum_scatter(
        lax.dot_general(
            hidden, scaled, (((0,), (0,)), ((), ())), preferred_element_type=jnp.float32
        ).astype(jnp.bfloat16),
        ("zl", "c"),
        scatter_dimension=0,
        tiled=True,
    ).astype(jnp.float32)
    return grads[None]


def solution(mesh):
    fine = Mesh(mesh.devices.reshape(4, 2, 4, 4, 4), ("zl", "c", "x", "zh", "y"))
    rows = P(("zl", "c", "x", "zh", "y"), None)
    split = P(("x", "zh", "y"), ("zl", "c"), None)
    in_specs = (rows, rows, split, split, rows, rows, P())
    return jax.shard_map(shards, mesh=fine, in_specs=in_specs, out_specs=split, check_vma=False)
```

```python
import functools

import jax
import jax.numpy as jnp
from jax import lax
from jax.experimental import pallas as pl
from jax.experimental.pallas import tpu as pltpu
from jax.sharding import Mesh, PartitionSpec as P

PLANE = ("x", "y")
RANKS = 8


def route_kernel(count, weighted, scale_ref, flags_ref, place_ref, *refs):
    metas, rows, out_ref, pick_ref = refs[:count], refs[count : 2 * count], refs[2 * count], refs[2 * count + 1]
    tok_count = metas[0].shape[0]
    slots = pick_ref.shape[2]

    @pl.when(pl.program_id(0) == 0)
    def _():
        lane = lax.broadcasted_iota(jnp.int32, (1, slots), 1)
        expert = jnp.zeros((1, slots), jnp.int32)
        for j in range(16):
            home = (j // 4) * 16 + place_ref[0] * 4 + j % 4
            other = lax.rem(home + 32, 64)
            held = jnp.where(flags_ref[lax.rem(home, 32)] == 1, other, home)
            expert = jnp.where(lane // RANKS == j, held, expert)
        expert = expert.astype(jnp.float32)
        rank_of = (lane % RANKS).astype(jnp.float32)
        earlier = (
            lax.broadcasted_iota(jnp.int32, (tok_count, tok_count), 0)
            > lax.broadcasted_iota(jnp.int32, (tok_count, tok_count), 1)
        ).astype(jnp.bfloat16)
        for s in range(count):
            meta = metas[s][...].astype(jnp.float32)
            chosen = jnp.zeros((tok_count, slots), jnp.float32)
            weight = jnp.zeros((tok_count, slots), jnp.float32)
            for k in range(6):
                hit = meta[:, k : k + 1] == expert
                chosen = jnp.where(hit, 1.0, chosen)
                if weighted:
                    weight = jnp.where(hit, meta[:, 6 + k : 7 + k] * scale_ref[0], weight)
            before = jnp.dot(earlier, chosen.astype(jnp.bfloat16), preferred_element_type=jnp.float32)
            value = weight if weighted else chosen
            pick_ref[s] = jnp.where((before == rank_of) & (chosen > 0.0), value, 0.0).astype(jnp.bfloat16)

    for s in range(count):
        picked = lax.dot_general(
            pick_ref[s], rows[s][...], (((0,), (0,)), ((), ())), preferred_element_type=jnp.float32
        )
        width = picked.shape[1]
        out_ref[:, s * RANKS : (s + 1) * RANKS, :] = picked.reshape(16, RANKS, width).astype(jnp.bfloat16)


def route(flags, place, metas, rows, width, weighted):
    count = len(rows)
    tok_count = rows[0].shape[0]
    tile = 512
    meta_block = width // 128
    smem = pl.BlockSpec(memory_space=pltpu.SMEM)
    scale = jnp.full((1,), 1.0 / 64.0, jnp.float32)
    return pl.pallas_call(
        functools.partial(route_kernel, count, weighted),
        grid=(width // tile,),
        in_specs=[smem] * 3
        + [pl.BlockSpec((tok_count, 128), lambda i: (0, meta_block))] * count
        + [pl.BlockSpec((tok_count, tile), lambda i: (0, i))] * count,
        out_specs=pl.BlockSpec((16, count * RANKS, tile), lambda i: (0, 0, i)),
        out_shape=jax.ShapeDtypeStruct((16, count * RANKS, width), jnp.bfloat16),
        scratch_shapes=[pltpu.VMEM((count, tok_count, 16 * RANKS), jnp.bfloat16)],
        cost_estimate=pl.CostEstimate(
            flops=2 * count * tok_count * 128 * width,
            bytes_accessed=count * (tok_count + 128) * width * 2,
            transcendentals=0,
        ),
    )(scale, flags, place, *metas, *rows)


def compute_kernel(count, starts_ref, x_ref, y_ref, *refs):
    parts, out_ref, full, hidden, sem = refs[:count], refs[count], refs[count + 1], refs[count + 2], refs[count + 3]
    copies = []
    for p in range(count):
        rows = parts[p].shape[0]
        start = pl.multiple_of(starts_ref[p], 16)
        copies.append(pltpu.make_async_copy(parts[p], full.at[pl.ds(start, rows), :], sem.at[p]))
        copies[-1].start()
    for copy in copies:
        copy.wait()
    units = hidden.shape[1]
    tile = 256
    for n in range(units // tile):
        gate = jnp.dot(x_ref[...], full[:, n * tile : (n + 1) * tile], preferred_element_type=jnp.float32)
        upper = jnp.dot(
            x_ref[...], full[:, units + n * tile : units + (n + 1) * tile], preferred_element_type=jnp.float32
        )
        hidden[:, n * tile : (n + 1) * tile] = (jax.nn.silu(gate) * upper).astype(jnp.bfloat16)
    wide = 512
    for d in range(y_ref.shape[1] // wide):
        out_ref[:, d * wide : (d + 1) * wide] = lax.dot_general(
            hidden[...],
            y_ref[:, d * wide : (d + 1) * wide],
            (((0,), (0,)), ((), ())),
            preferred_element_type=jnp.float32,
        ).astype(jnp.bfloat16)


def compute(starts, x_rows, y_rows, parts):
    rows, width = x_rows.shape
    both = parts[0].shape[1]
    count = len(parts)
    vmem = pl.BlockSpec(memory_space=pltpu.VMEM)
    return pl.pallas_call(
        functools.partial(compute_kernel, count),
        in_specs=[pl.BlockSpec(memory_space=pltpu.SMEM), vmem, vmem] + [pl.BlockSpec(memory_space=pl.ANY)] * count,
        out_specs=vmem,
        out_shape=jax.ShapeDtypeStruct((both // 2, width), jnp.bfloat16),
        scratch_shapes=[
            pltpu.VMEM((width, both), jnp.bfloat16),
            pltpu.VMEM((rows, both // 2), jnp.bfloat16),
            pltpu.SemaphoreType.DMA((count,)),
        ],
        compiler_params=pltpu.CompilerParams(vmem_limit_bytes=40 << 20),
        cost_estimate=pl.CostEstimate(
            flops=3 * rows * both * width, bytes_accessed=width * both * 2 + rows * width * 4, transcendentals=rows * both // 2
        ),
    )(starts, x_rows, y_rows, *parts)


def plane_exchange(value):
    got = lax.all_to_all(value, PLANE, split_axis=0, concat_axis=0, tiled=True)
    return got.reshape(-1, value.shape[2])


def together(*values):
    return lax.optimization_barrier(values)


def shards(tokens, cotangent, w_gate, w_up, expert_ids, gate_num, swap_flags):
    width = tokens.shape[1]
    half = tokens.shape[0] // 2
    ahead, back = [(i, (i + 1) % 4) for i in range(4)], [(i, (i - 1) % 4) for i in range(4)]
    opposite = [(i, (i + 2) % 4) for i in range(4)]
    cores = [(0, 1), (1, 0)]
    place, line, core = lax.axis_index("zh"), lax.axis_index("zl"), lax.axis_index("c")
    me = (lax.axis_index("x") * 4 + place) * 4 + lax.axis_index("y")
    place = place.reshape(1)
    send = functools.partial(route, swap_flags, place, width=width)
    meta = jnp.concatenate([expert_ids, gate_num], axis=1).astype(jnp.bfloat16)
    meta = jnp.pad(meta, ((0, 0), (0, 128 - meta.shape[1])))
    tok = jnp.concatenate([tokens, meta], axis=1)
    weights = jnp.concatenate([w_gate[0], w_up[0]], axis=1)
    tok_l, tok_r, other = together(
        lax.ppermute(tok, "zh", ahead), lax.ppermute(tok, "zh", back), lax.ppermute(weights, "x", opposite)
    )
    weights = jnp.where(swap_flags[me % 32] == 1, other, weights)
    cot, tok_l, tok_r = together(cotangent, tok_l, tok_r)
    tok_fl, tok_fr, cot_l, cot_r, weights = together(
        lax.ppermute(tok_l[:half], "zh", ahead),
        lax.ppermute(tok_r[half:], "zh", back),
        lax.ppermute(cot, "zh", ahead),
        lax.ppermute(cot, "zh", back),
        weights,
    )
    tok_o = jnp.concatenate([tok_fl, tok_fr], axis=0)
    toks = [tok, tok_l, tok_r, tok_o]
    x_rows = plane_exchange(send(toks, toks, weighted=False))
    deep = weights.shape[0] // 2
    upper_half, lower_half = weights[:deep], weights[deep:]
    cot_fl, cot_fr, w_lu, w_rd, w_c = together(
        lax.ppermute(cot_l[:half], "zh", ahead),
        lax.ppermute(cot_r[half:], "zh", back),
        lax.ppermute(upper_half, "zl", ahead),
        lax.ppermute(lower_half, "zl", back),
        lax.ppermute(weights, "c", cores),
    )
    y_send = send(toks, [cot, cot_l, cot_r, jnp.concatenate([cot_fl, cot_fr], axis=0)], weighted=True)
    upper_half, lower_half, y_send = together(upper_half, lower_half, y_send)
    y_rows = plane_exchange(y_send)
    w_ld, w_ru, w_fl, w_fr, w_luc, w_rdc = together(
        lax.ppermute(lower_half, "zl", ahead),
        lax.ppermute(upper_half, "zl", back),
        lax.ppermute(w_lu, "zl", ahead),
        lax.ppermute(w_rd, "zl", back),
        lax.ppermute(w_lu, "c", cores),
        lax.ppermute(w_rd, "c", cores),
    )
    late = [lax.ppermute(value, "c", cores) for value in (w_ld, w_ru, w_fl, w_fr)]
    parts = [weights, w_lu, w_rd, w_ld, w_ru, w_fl, w_fr, w_c, w_luc, w_rdc, *late]
    away = jnp.array([0, 3, 1, 3, 1, 2, 2], jnp.int32)
    extra = jnp.array([0, 0, deep, deep, 0, 0, deep], jnp.int32)
    block = (line + away) % 4 * 2
    starts = jnp.concatenate([(block + core) * 2 * deep + extra, (block + 1 - core) * 2 * deep + extra])
    partial = compute(starts, x_rows, y_rows, parts)
    grads = lax.psum_scatter(partial, ("zl", "c"), scatter_dimension=0, tiled=True).astype(jnp.float32)
    return grads[None]


def solution(mesh):
    fine = Mesh(mesh.devices.reshape(4, 2, 4, 4, 4), ("zl", "c", "x", "zh", "y"))
    rows = P(("zl", "c", "x", "zh", "y"), None)
    split = P(("x", "zh", "y"), ("zl", "c"), None)
    in_specs = (rows, rows, split, split, rows, rows, P())
    return jax.shard_map(shards, mesh=fine, in_specs=in_specs, out_specs=split, check_vma=False)
```

```python
import functools

import jax
import jax.numpy as jnp
from jax import lax
from jax.experimental import pallas as pl
from jax.experimental.pallas import tpu as pltpu
from jax.sharding import Mesh, PartitionSpec as P

PLANE = ("x", "y")
RANKS = 8


def route_kernel(count, flags_ref, place_ref, *refs):
    metas, xs, ys = refs[:count], refs[count : 2 * count], refs[2 * count : 3 * count]
    out_ref, pick_ref, weigh_ref = refs[3 * count :]
    tok_count = metas[0].shape[0]
    slots = pick_ref.shape[2]

    @pl.when(pl.program_id(0) == 0)
    def _():
        lane = lax.broadcasted_iota(jnp.int32, (1, slots), 1)
        expert = jnp.zeros((1, slots), jnp.int32)
        for j in range(16):
            home = (j // 4) * 16 + place_ref[0] * 4 + j % 4
            other = lax.rem(home + 32, 64)
            held = jnp.where(flags_ref[lax.rem(home, 32)] == 1, other, home)
            expert = jnp.where(lane // RANKS == j, held, expert)
        expert = expert.astype(jnp.float32)
        rank_of = (lane % RANKS).astype(jnp.float32)
        earlier = (
            lax.broadcasted_iota(jnp.int32, (tok_count, tok_count), 0)
            > lax.broadcasted_iota(jnp.int32, (tok_count, tok_count), 1)
        ).astype(jnp.bfloat16)
        for s in range(count):
            meta = metas[s][...].astype(jnp.float32)
            weight = jnp.zeros((tok_count, slots), jnp.float32)
            for k in range(6):
                weight = jnp.where(meta[:, k : k + 1] == expert, meta[:, 6 + k : 7 + k], weight)
            chosen = jnp.where(weight > 0.0, 1.0, 0.0)
            before = jnp.dot(earlier, chosen.astype(jnp.bfloat16), preferred_element_type=jnp.float32)
            here = before == rank_of
            pick_ref[s] = jnp.where(here, chosen, 0.0).astype(jnp.bfloat16)
            weigh_ref[s] = jnp.where(here, weight * (1.0 / 64.0), 0.0).astype(jnp.bfloat16)

    for base, picks, rows in ((0, pick_ref, xs), (count, weigh_ref, ys)):
        for s in range(count):
            picked = lax.dot_general(
                picks[s], rows[s][...], (((0,), (0,)), ((), ())), preferred_element_type=jnp.float32
            )
            at = (base + s) * RANKS
            out_ref[:, at : at + RANKS, :] = picked.reshape(16, RANKS, picked.shape[1]).astype(jnp.bfloat16)


def route(flags, place, width, sources):
    count = len(sources)
    tok_count = 64
    tile = 512
    meta_block = width // 128
    smem = pl.BlockSpec(memory_space=pltpu.SMEM)
    x_of, y_of = [pair[0] for pair in sources], [pair[1] for pair in sources]
    y_block = 1 if x_of[0] is y_of[0] else 0
    return pl.pallas_call(
        functools.partial(route_kernel, count),
        grid=(width // tile,),
        in_specs=[smem] * 2
        + [pl.BlockSpec((tok_count, 128), lambda i: (0, meta_block))] * count
        + [pl.BlockSpec((tok_count, tile), lambda i: (0, i))] * count
        + [pl.BlockSpec((tok_count, tile), lambda i: (y_block, i))] * count,
        out_specs=pl.BlockSpec((16, 2 * count * RANKS, tile), lambda i: (0, 0, i)),
        out_shape=jax.ShapeDtypeStruct((16, 2 * count * RANKS, width), jnp.bfloat16),
        scratch_shapes=[pltpu.VMEM((count, tok_count, 16 * RANKS), jnp.bfloat16)] * 2,
        cost_estimate=pl.CostEstimate(
            flops=4 * count * tok_count * 128 * width,
            bytes_accessed=2 * count * (tok_count + 128) * width * 2,
            transcendentals=0,
        ),
    )(flags, place, *x_of, *x_of, *y_of)


def compute_kernel(starts_ref, *refs):
    near, far, blocks = refs[0:2], refs[2:4], refs[4:9]
    out_ref, x_near, x_far, y_near, y_far, full, hidden, sem = refs[9:]
    near_rows, far_rows = near[0].shape[1] // 2, far[0].shape[1] // 2
    copies = []

    def begin(source, target):
        copies.append(pltpu.make_async_copy(source, target, sem.at[len(copies)]))
        copies[-1].start()

    deep = blocks[3].shape[0]
    for b in range(5):
        for part in range(blocks[b].shape[0] // deep):
            start = pl.multiple_of(starts_ref[(2 * b + part) if b < 3 else 3 + b], 16)
            begin(blocks[b].at[part * deep : (part + 1) * deep, :], full.at[pl.ds(start, deep), :])
    for core in range(2):
        begin(near[core].at[:, :near_rows, :], x_near.at[core])
        begin(far[core].at[:, :far_rows, :], x_far.at[core])
    for core in range(2):
        begin(near[core].at[:, near_rows:, :], y_near.at[core])
        begin(far[core].at[:, far_rows:, :], y_far.at[core])
    for copy in copies[:-4]:
        copy.wait()
    width, both = full.shape
    units = both // 2
    n_near, n_far = 32 * near_rows, 32 * far_rows
    at = 0
    tile = 256
    for rows, total in ((x_near.reshape(n_near, width), n_near), (x_far.reshape(n_far, width), n_far)):
        for m in range(total // tile):
            sums = jnp.dot(rows[m * tile : (m + 1) * tile, :], full[...], preferred_element_type=jnp.float32)
            hidden[at : at + tile, :] = (jax.nn.silu(sums[:, :units]) * sums[:, units:]).astype(jnp.bfloat16)
            at += tile
    for copy in copies[-4:]:
        copy.wait()
    wide = 512
    y_n, y_f = y_near.reshape(n_near, width), y_far.reshape(n_far, width)
    for d in range(width // wide):
        cols = slice(d * wide, (d + 1) * wide)
        over_rows = (((0,), (0,)), ((), ()))
        sums = lax.dot_general(hidden[:n_near, :], y_n[:, cols], over_rows, preferred_element_type=jnp.float32)
        sums += lax.dot_general(hidden[n_near:, :], y_f[:, cols], over_rows, preferred_element_type=jnp.float32)
        out_ref[:, cols] = sums.astype(jnp.bfloat16)


def compute(starts, near, far, blocks):
    width, both = near[0].shape[2], blocks[0].shape[1]
    near_rows, far_rows = near[0].shape[1] // 2, far[0].shape[1] // 2
    rows = 32 * (near_rows + far_rows)
    hbm = pl.BlockSpec(memory_space=pltpu.HBM)
    return pl.pallas_call(
        compute_kernel,
        in_specs=[pl.BlockSpec(memory_space=pltpu.SMEM)] + [hbm] * 9,
        out_specs=pl.BlockSpec(memory_space=pltpu.VMEM),
        out_shape=jax.ShapeDtypeStruct((both // 2, width), jnp.bfloat16),
        scratch_shapes=[
            pltpu.VMEM((2, 16, near_rows, width), jnp.bfloat16),
            pltpu.VMEM((2, 16, far_rows, width), jnp.bfloat16),
            pltpu.VMEM((2, 16, near_rows, width), jnp.bfloat16),
            pltpu.VMEM((2, 16, far_rows, width), jnp.bfloat16),
            pltpu.VMEM((width, both), jnp.bfloat16),
            pltpu.VMEM((rows, both // 2), jnp.bfloat16),
            pltpu.SemaphoreType.DMA((16,)),
        ],
        compiler_params=pltpu.CompilerParams(vmem_limit_bytes=60 << 20),
        cost_estimate=pl.CostEstimate(
            flops=3 * rows * both * width, bytes_accessed=width * both * 2 + rows * width * 4, transcendentals=rows * both // 2
        ),
    )(starts, *near, *far, *blocks)


def pack_kernel(flag_ref, core_ref, gate_ref, up_ref, other_gate_ref, other_up_ref, mine_ref, theirs_ref):
    swapped = flag_ref[0] == 1
    units = gate_ref.shape[1]
    unit = lax.broadcasted_iota(jnp.int32, (units, units // 2), 0)
    column = lax.broadcasted_iota(jnp.int32, (units, units // 2), 1)
    for target, core in ((mine_ref, core_ref[0]), (theirs_ref, 1 - core_ref[0])):
        chosen = (unit == (column // 96 * 2 + core) * 96 + column % 96).astype(jnp.bfloat16)
        for at, here, there in ((0, gate_ref, other_gate_ref), (1, up_ref, other_up_ref)):
            held = jnp.where(swapped, there[...], here[...])
            target[:, at * units // 2 : (at + 1) * units // 2] = jnp.dot(
                held, chosen, preferred_element_type=jnp.float32
            ).astype(jnp.bfloat16)


def pack(flag, core, *matrices):
    smem, vmem = pl.BlockSpec(memory_space=pltpu.SMEM), pl.BlockSpec(memory_space=pltpu.VMEM)
    shape = jax.ShapeDtypeStruct(matrices[0].shape, jnp.bfloat16)
    return pl.pallas_call(
        pack_kernel, in_specs=[smem] * 2 + [vmem] * 4, out_specs=[vmem] * 2, out_shape=[shape] * 2
    )(flag, core, *matrices)


def together(*values):
    return lax.optimization_barrier(values)


def shards(tokens, cotangent, w_gate, w_up, expert_ids, gate_num, swap_flags):
    tok_count, width = tokens.shape
    ahead, back = [(i, (i + 1) % 4) for i in range(4)], [(i, (i - 1) % 4) for i in range(4)]
    opposite = [(i, (i + 2) % 4) for i in range(4)]
    cores = [(0, 1), (1, 0)]
    place, line, core = lax.axis_index("zh"), lax.axis_index("zl"), lax.axis_index("c")
    me = (lax.axis_index("x") * 4 + place) * 4 + lax.axis_index("y")
    place = place.reshape(1)
    meta = jnp.concatenate([expert_ids, gate_num], axis=1).astype(jnp.bfloat16)
    meta = jnp.pad(meta, ((0, tok_count), (0, 128 - meta.shape[1])))
    own = jnp.concatenate([jnp.concatenate([tokens, cotangent], axis=0), meta], axis=1)
    deep = w_gate.shape[1]
    from_l, from_r, other_gate, other_up = together(
        lax.ppermute(own, "zh", ahead),
        lax.ppermute(own, "zh", back),
        lax.ppermute(w_gate[0], "x", opposite),
        lax.ppermute(w_up[0], "x", opposite),
    )
    flag = lax.dynamic_slice(swap_flags, (me % 32,), (1,))
    mine, theirs = pack(flag, core.reshape(1), w_gate[0], w_up[0], other_gate, other_up)
    block = jnp.concatenate([mine, lax.ppermute(theirs, "c", cores)], axis=0)
    near = lax.all_to_all(
        route(swap_flags, place, width, [(own, own), (from_l, from_l), (from_r, from_r)]), PLANE, 0, 0, tiled=True
    )
    near, tok_o, cot_o, block_l, block_r = together(
        near,
        lax.ppermute(from_l[:tok_count], "zh", ahead),
        lax.ppermute(from_r[tok_count:], "zh", back),
        lax.ppermute(block, "zl", ahead),
        lax.ppermute(block, "zl", back),
    )
    far, block_fl, block_fr, near_c = together(
        lax.all_to_all(route(swap_flags, place, width, [(tok_o, cot_o)]), PLANE, 0, 0, tiled=True),
        lax.ppermute(block_l[:deep], "zl", ahead),
        lax.ppermute(block_r[deep:], "zl", back),
        lax.ppermute(near, "c", cores),
    )
    far_c = lax.ppermute(far, "c", cores)
    away = jnp.array([0, 0, 3, 3, 1, 1, 2, 2], jnp.int32)
    which = jnp.array([0, 1, 0, 1, 0, 1, 0, 1], jnp.int32)
    starts = (2 * ((line + away) % 4) + (core + which) % 2) * deep
    partial = compute(starts, [near, near_c], [far, far_c], [block, block_l, block_r, block_fl, block_fr])
    return lax.psum_scatter(partial, "zl", scatter_dimension=0, tiled=True).astype(jnp.float32)[None]


def solution(mesh):
    fine = Mesh(mesh.devices.reshape(4, 2, 4, 4, 4), ("zl", "c", "x", "zh", "y"))
    rows = P(("zl", "c", "x", "zh", "y"), None)
    split = P(("x", "zh", "y"), ("zl", "c"), None)
    in_specs = (rows, rows, split, split, rows, rows, P())
    return jax.shard_map(shards, mesh=fine, in_specs=in_specs, out_specs=split, check_vma=False)
```

```python
import functools

import jax
import jax.numpy as jnp
from jax import lax
from jax.experimental import pallas as pl
from jax.experimental.pallas import tpu as pltpu
from jax.sharding import Mesh, PartitionSpec as P

PLANE = ("x", "y")
RANKS = 8


def route_kernel(count, flags_ref, place_ref, *refs):
    metas, xs, ys = refs[:count], refs[count : 2 * count], refs[2 * count : 3 * count]
    out_ref, pick_ref, weigh_ref = refs[3 * count :]
    tok_count = metas[0].shape[0]
    slots = pick_ref.shape[2]

    @pl.when(pl.program_id(0) == 0)
    def _():
        lane = lax.broadcasted_iota(jnp.int32, (1, slots), 1)
        expert = jnp.zeros((1, slots), jnp.int32)
        for j in range(16):
            home = (j // 4) * 16 + place_ref[0] * 4 + j % 4
            other = lax.rem(home + 32, 64)
            held = jnp.where(flags_ref[lax.rem(home, 32)] == 1, other, home)
            expert = jnp.where(lane // RANKS == j, held, expert)
        expert = expert.astype(jnp.float32)
        rank_of = (lane % RANKS).astype(jnp.float32)
        earlier = (
            lax.broadcasted_iota(jnp.int32, (tok_count, tok_count), 0)
            > lax.broadcasted_iota(jnp.int32, (tok_count, tok_count), 1)
        ).astype(jnp.bfloat16)
        for s in range(count):
            meta = metas[s][...].astype(jnp.float32)
            weight = jnp.zeros((tok_count, slots), jnp.float32)
            for k in range(6):
                weight = jnp.where(meta[:, k : k + 1] == expert, meta[:, 6 + k : 7 + k], weight)
            chosen = jnp.where(weight > 0.0, 1.0, 0.0)
            before = jnp.dot(earlier, chosen.astype(jnp.bfloat16), preferred_element_type=jnp.float32)
            here = before == rank_of
            pick_ref[s] = jnp.where(here, chosen, 0.0).astype(jnp.bfloat16)
            weigh_ref[s] = jnp.where(here, weight * (1.0 / 64.0), 0.0).astype(jnp.bfloat16)

    for base, picks, rows in ((0, pick_ref, xs), (count, weigh_ref, ys)):
        for s in range(count):
            picked = lax.dot_general(
                picks[s], rows[s][...], (((0,), (0,)), ((), ())), preferred_element_type=jnp.float32
            )
            at = (base + s) * RANKS
            out_ref[:, at : at + RANKS, :] = picked.reshape(16, RANKS, picked.shape[1]).astype(jnp.bfloat16)


def route(flags, place, width, sources):
    count = len(sources)
    tok_count = 64
    tile = 512
    meta_block = width // 128
    smem = pl.BlockSpec(memory_space=pltpu.SMEM)
    x_of, y_of = [pair[0] for pair in sources], [pair[1] for pair in sources]
    y_block = 1 if x_of[0] is y_of[0] else 0
    return pl.pallas_call(
        functools.partial(route_kernel, count),
        grid=(width // tile,),
        in_specs=[smem] * 2
        + [pl.BlockSpec((tok_count, 128), lambda i: (0, meta_block))] * count
        + [pl.BlockSpec((tok_count, tile), lambda i: (0, i))] * count
        + [pl.BlockSpec((tok_count, tile), lambda i: (y_block, i))] * count,
        out_specs=pl.BlockSpec((16, 2 * count * RANKS, tile), lambda i: (0, 0, i)),
        out_shape=jax.ShapeDtypeStruct((16, 2 * count * RANKS, width), jnp.bfloat16),
        scratch_shapes=[pltpu.VMEM((count, tok_count, 16 * RANKS), jnp.bfloat16)] * 2,
        cost_estimate=pl.CostEstimate(
            flops=4 * count * tok_count * 128 * width,
            bytes_accessed=2 * count * (tok_count + 128) * width * 2,
            transcendentals=0,
        ),
    )(flags, place, *x_of, *x_of, *y_of)


def compute_kernel(starts_ref, *refs):
    near, far, blocks = refs[0:2], refs[2:4], refs[4:9]
    out_ref, x_near, x_far, y_near, y_far, full, hidden, sem = refs[9:]
    near_rows, far_rows = near[0].shape[1] // 2, far[0].shape[1] // 2
    copies = []

    def begin(source, target):
        copies.append(pltpu.make_async_copy(source, target, sem.at[len(copies)]))
        copies[-1].start()

    deep = blocks[3].shape[0]
    for b in range(5):
        for part in range(blocks[b].shape[0] // deep):
            start = pl.multiple_of(starts_ref[(2 * b + part) if b < 3 else 3 + b], 16)
            begin(blocks[b].at[part * deep : (part + 1) * deep, :], full.at[pl.ds(start, deep), :])
    for core in range(2):
        begin(near[core].at[:, :near_rows, :], x_near.at[core])
        begin(far[core].at[:, :far_rows, :], x_far.at[core])
    for core in range(2):
        begin(near[core].at[:, near_rows:, :], y_near.at[core])
        begin(far[core].at[:, far_rows:, :], y_far.at[core])
    for copy in copies[:-4]:
        copy.wait()
    width, both = full.shape
    units = both // 2
    n_near, n_far = 32 * near_rows, 32 * far_rows
    at = 0
    tile = 256
    for rows, total in ((x_near.reshape(n_near, width), n_near), (x_far.reshape(n_far, width), n_far)):
        for m in range(total // tile):
            sums = jnp.dot(rows[m * tile : (m + 1) * tile, :], full[...], preferred_element_type=jnp.float32)
            hidden[at : at + tile, :] = (jax.nn.silu(sums[:, :units]) * sums[:, units:]).astype(jnp.bfloat16)
            at += tile
    for copy in copies[-4:]:
        copy.wait()
    wide = 512
    y_n, y_f = y_near.reshape(n_near, width), y_far.reshape(n_far, width)
    for d in range(width // wide):
        cols = slice(d * wide, (d + 1) * wide)
        over_rows = (((0,), (0,)), ((), ()))
        sums = lax.dot_general(hidden[:n_near, :], y_n[:, cols], over_rows, preferred_element_type=jnp.float32)
        sums += lax.dot_general(hidden[n_near:, :], y_f[:, cols], over_rows, preferred_element_type=jnp.float32)
        out_ref[:, cols] = sums.astype(jnp.bfloat16)


def compute(starts, near, far, blocks):
    width, both = near[0].shape[2], blocks[0].shape[1]
    near_rows, far_rows = near[0].shape[1] // 2, far[0].shape[1] // 2
    rows = 32 * (near_rows + far_rows)
    hbm = pl.BlockSpec(memory_space=pltpu.HBM)
    return pl.pallas_call(
        compute_kernel,
        in_specs=[pl.BlockSpec(memory_space=pltpu.SMEM)] + [hbm] * 9,
        out_specs=pl.BlockSpec(memory_space=pltpu.VMEM),
        out_shape=jax.ShapeDtypeStruct((both // 2, width), jnp.bfloat16),
        scratch_shapes=[
            pltpu.VMEM((2, 16, near_rows, width), jnp.bfloat16),
            pltpu.VMEM((2, 16, far_rows, width), jnp.bfloat16),
            pltpu.VMEM((2, 16, near_rows, width), jnp.bfloat16),
            pltpu.VMEM((2, 16, far_rows, width), jnp.bfloat16),
            pltpu.VMEM((width, both), jnp.bfloat16),
            pltpu.VMEM((rows, both // 2), jnp.bfloat16),
            pltpu.SemaphoreType.DMA((16,)),
        ],
        compiler_params=pltpu.CompilerParams(vmem_limit_bytes=60 << 20),
        cost_estimate=pl.CostEstimate(
            flops=3 * rows * both * width, bytes_accessed=width * both * 2 + rows * width * 4, transcendentals=rows * both // 2
        ),
    )(starts, *near, *far, *blocks)


def pack_kernel(flag_ref, core_ref, gate_ref, up_ref, other_gate_ref, other_up_ref, mine_ref, theirs_ref):
    swapped = flag_ref[0] == 1
    units = gate_ref.shape[1]
    unit = lax.broadcasted_iota(jnp.int32, (units, units // 2), 0)
    column = lax.broadcasted_iota(jnp.int32, (units, units // 2), 1)
    for target, core in ((mine_ref, core_ref[0]), (theirs_ref, 1 - core_ref[0])):
        chosen = (unit == (column // 96 * 2 + core) * 96 + column % 96).astype(jnp.bfloat16)
        for at, here, there in ((0, gate_ref, other_gate_ref), (1, up_ref, other_up_ref)):
            held = jnp.where(swapped, there[...], here[...])
            target[:, at * units // 2 : (at + 1) * units // 2] = jnp.dot(
                held, chosen, preferred_element_type=jnp.float32
            ).astype(jnp.bfloat16)


def pack(flag, core, *matrices):
    smem, vmem = pl.BlockSpec(memory_space=pltpu.SMEM), pl.BlockSpec(memory_space=pltpu.VMEM)
    shape = jax.ShapeDtypeStruct(matrices[0].shape, jnp.bfloat16)
    return pl.pallas_call(
        pack_kernel, in_specs=[smem] * 2 + [vmem] * 4, out_specs=[vmem] * 2, out_shape=[shape] * 2
    )(flag, core, *matrices)


def together(*values):
    return lax.optimization_barrier(values)


def z_steps(step_of):
    pairs = []
    for line in range(4):
        to, by = step_of[line]
        pairs += [(line * 4 + hi, to * 4 + (hi + by) % 4) for hi in range(4)]
    return pairs


def shards(tokens, cotangent, w_gate, w_up, expert_ids, gate_num, swap_flags):
    tok_count, width = tokens.shape
    deep = w_gate.shape[1]
    ahead, back = [(i, (i + 1) % 4) for i in range(4)], [(i, (i - 1) % 4) for i in range(4)]
    opposite = [(i, (i + 2) % 4) for i in range(4)]
    cores = [(0, 1), (1, 0)]
    along_z = ("zl", "zh")
    first = z_steps([(0, 1), (2, -1), (1, 1), (3, -1)])
    second = z_steps([(2, -1), (0, 1), (3, -1), (1, 1)])
    onward = z_steps([(0, 1), (1, 1), (2, -1), (3, -1)])
    place, line, core = lax.axis_index("zh"), lax.axis_index("zl"), lax.axis_index("c")
    me = (lax.axis_index("x") * 4 + place) * 4 + lax.axis_index("y")
    select = functools.partial(route, swap_flags, place.reshape(1), width)
    meta = jnp.concatenate([expert_ids, gate_num], axis=1).astype(jnp.bfloat16)
    meta = jnp.pad(meta, ((0, tok_count), (0, 128 - meta.shape[1])))
    own = jnp.concatenate([jnp.concatenate([tokens, cotangent], axis=0), meta], axis=1)
    rows_a, rows_b = lax.ppermute(own, along_z, first), lax.ppermute(own, along_z, second)
    flag = lax.dynamic_slice(swap_flags, (me % 32,), (1,))
    mine, theirs = pack(
        flag,
        core.reshape(1),
        w_gate[0],
        w_up[0],
        lax.ppermute(w_gate[0], "x", opposite),
        lax.ppermute(w_up[0], "x", opposite),
    )
    block = jnp.concatenate([mine, lax.ppermute(theirs, "c", cores)], axis=0)
    rows_a, rows_b, block, block_l = together(rows_a, rows_b, block, lax.ppermute(block, "zl", ahead))
    near, rows_f, block_r, block_fl = together(
        lax.all_to_all(select([(own, own), (rows_a, rows_a), (rows_b, rows_b)]), PLANE, 0, 0, tiled=True),
        lax.ppermute(rows_a, along_z, onward),
        lax.ppermute(block, "zl", back),
        lax.ppermute(block_l[:deep], "zl", ahead),
    )
    far, block_fr, near_c = together(
        lax.all_to_all(select([(rows_f, rows_f)]), PLANE, 0, 0, tiled=True),
        lax.ppermute(block_r[deep:], "zl", back),
        lax.ppermute(near, "c", cores),
    )
    far_c = lax.ppermute(far, "c", cores)
    away = jnp.array([0, 0, 3, 3, 1, 1, 2, 2], jnp.int32)
    which = jnp.array([0, 1, 0, 1, 0, 1, 0, 1], jnp.int32)
    starts = (2 * ((line + away) % 4) + (core + which) % 2) * deep
    partial = compute(starts, [near, near_c], [far, far_c], [block, block_l, block_r, block_fl, block_fr])
    return lax.psum_scatter(partial, "zl", scatter_dimension=0, tiled=True).astype(jnp.float32)[None]


def solution(mesh):
    fine = Mesh(mesh.devices.reshape(4, 2, 4, 4, 4), ("zl", "c", "x", "zh", "y"))
    rows = P(("zl", "c", "x", "zh", "y"), None)
    split = P(("x", "zh", "y"), ("zl", "c"), None)
    in_specs = (rows, rows, split, split, rows, rows, P())
    return jax.shard_map(shards, mesh=fine, in_specs=in_specs, out_specs=split, check_vma=False)
```

```python
import functools

import jax
import jax.numpy as jnp
from jax import lax
from jax.experimental import pallas as pl
from jax.experimental.pallas import tpu as pltpu
from jax.sharding import Mesh, PartitionSpec as P

PLANE = ("x", "y")
RANKS = 8


def route_kernel(count, flags_ref, place_ref, *refs):
    metas, xs, ys = refs[:count], refs[count : 2 * count], refs[2 * count : 3 * count]
    out_ref, pick_ref, weigh_ref = refs[3 * count :]
    tok_count = metas[0].shape[0]
    slots = pick_ref.shape[2]

    @pl.when(pl.program_id(0) == 0)
    def _():
        lane = lax.broadcasted_iota(jnp.int32, (1, slots), 1)
        expert = jnp.zeros((1, slots), jnp.int32)
        for j in range(16):
            home = (j // 4) * 16 + place_ref[0] * 4 + j % 4
            other = lax.rem(home + 32, 64)
            held = jnp.where(flags_ref[lax.rem(home, 32)] == 1, other, home)
            expert = jnp.where(lane // RANKS == j, held, expert)
        expert = expert.astype(jnp.float32)
        rank_of = (lane % RANKS).astype(jnp.float32)
        earlier = (
            lax.broadcasted_iota(jnp.int32, (tok_count, tok_count), 0)
            > lax.broadcasted_iota(jnp.int32, (tok_count, tok_count), 1)
        ).astype(jnp.bfloat16)
        for s in range(count):
            meta = metas[s][...].astype(jnp.float32)
            weight = jnp.zeros((tok_count, slots), jnp.float32)
            for k in range(6):
                weight = jnp.where(meta[:, k : k + 1] == expert, meta[:, 6 + k : 7 + k], weight)
            chosen = jnp.where(weight > 0.0, 1.0, 0.0)
            before = jnp.dot(earlier, chosen.astype(jnp.bfloat16), preferred_element_type=jnp.float32)
            here = before == rank_of
            pick_ref[s] = jnp.where(here, chosen, 0.0).astype(jnp.bfloat16)
            weigh_ref[s] = jnp.where(here, weight * (1.0 / 64.0), 0.0).astype(jnp.bfloat16)

    for base, picks, rows in ((0, pick_ref, xs), (count, weigh_ref, ys)):
        for s in range(count):
            picked = lax.dot_general(
                picks[s], rows[s][...], (((0,), (0,)), ((), ())), preferred_element_type=jnp.float32
            )
            at = (base + s) * RANKS
            out_ref[:, at : at + RANKS, :] = picked.reshape(16, RANKS, picked.shape[1]).astype(jnp.bfloat16)


def route(flags, place, width, sources):
    count = len(sources)
    tok_count = 64
    tile = 512
    meta_block = width // 128
    smem = pl.BlockSpec(memory_space=pltpu.SMEM)
    x_of, y_of = [pair[0] for pair in sources], [pair[1] for pair in sources]
    y_block = 1 if x_of[0] is y_of[0] else 0
    return pl.pallas_call(
        functools.partial(route_kernel, count),
        grid=(width // tile,),
        in_specs=[smem] * 2
        + [pl.BlockSpec((tok_count, 128), lambda i: (0, meta_block))] * count
        + [pl.BlockSpec((tok_count, tile), lambda i: (0, i))] * count
        + [pl.BlockSpec((tok_count, tile), lambda i: (y_block, i))] * count,
        out_specs=pl.BlockSpec((16, 2 * count * RANKS, tile), lambda i: (0, 0, i)),
        out_shape=jax.ShapeDtypeStruct((16, 2 * count * RANKS, width), jnp.bfloat16),
        scratch_shapes=[pltpu.VMEM((count, tok_count, 16 * RANKS), jnp.bfloat16)] * 2,
        cost_estimate=pl.CostEstimate(
            flops=40_000_000_000,
            bytes_accessed=2 * count * (tok_count + 128) * width * 2,
            transcendentals=0,
        ),
    )(flags, place, *x_of, *x_of, *y_of)


def compute_kernel(starts_ref, *refs):
    near, far, blocks = refs[0:2], refs[2:4], refs[4:9]
    out_ref, x_near, x_far, y_near, y_far, full, hidden, sem = refs[9:]
    near_rows, far_rows = near[0].shape[1] // 2, far[0].shape[1] // 2
    copies = []

    def begin(source, target):
        copies.append(pltpu.make_async_copy(source, target, sem.at[len(copies)]))
        copies[-1].start()

    deep = blocks[3].shape[0]
    for b in range(5):
        for part in range(blocks[b].shape[0] // deep):
            start = pl.multiple_of(starts_ref[(2 * b + part) if b < 3 else 3 + b], 16)
            begin(blocks[b].at[part * deep : (part + 1) * deep, :], full.at[pl.ds(start, deep), :])
    for core in range(2):
        begin(near[core].at[:, :near_rows, :], x_near.at[core])
        begin(far[core].at[:, :far_rows, :], x_far.at[core])
    for core in range(2):
        begin(near[core].at[:, near_rows:, :], y_near.at[core])
        begin(far[core].at[:, far_rows:, :], y_far.at[core])
    for copy in copies[:-4]:
        copy.wait()
    width, both = full.shape
    units = both // 2
    n_near, n_far = 32 * near_rows, 32 * far_rows
    at = 0
    tile = 256
    for rows, total in ((x_near.reshape(n_near, width), n_near), (x_far.reshape(n_far, width), n_far)):
        for m in range(total // tile):
            sums = jnp.dot(rows[m * tile : (m + 1) * tile, :], full[...], preferred_element_type=jnp.float32)
            hidden[at : at + tile, :] = (jax.nn.silu(sums[:, :units]) * sums[:, units:]).astype(jnp.bfloat16)
            at += tile
    for copy in copies[-4:]:
        copy.wait()
    wide = 512
    y_n, y_f = y_near.reshape(n_near, width), y_far.reshape(n_far, width)
    for d in range(width // wide):
        cols = slice(d * wide, (d + 1) * wide)
        over_rows = (((0,), (0,)), ((), ()))
        sums = lax.dot_general(hidden[:n_near, :], y_n[:, cols], over_rows, preferred_element_type=jnp.float32)
        sums += lax.dot_general(hidden[n_near:, :], y_f[:, cols], over_rows, preferred_element_type=jnp.float32)
        out_ref[:, cols] = sums.astype(jnp.bfloat16)


def compute(starts, near, far, blocks):
    width, both = near[0].shape[2], blocks[0].shape[1]
    near_rows, far_rows = near[0].shape[1] // 2, far[0].shape[1] // 2
    rows = 32 * (near_rows + far_rows)
    hbm = pl.BlockSpec(memory_space=pltpu.HBM)
    return pl.pallas_call(
        compute_kernel,
        in_specs=[pl.BlockSpec(memory_space=pltpu.SMEM)] + [hbm] * 9,
        out_specs=pl.BlockSpec(memory_space=pltpu.VMEM),
        out_shape=jax.ShapeDtypeStruct((both // 2, width), jnp.bfloat16),
        scratch_shapes=[
            pltpu.VMEM((2, 16, near_rows, width), jnp.bfloat16),
            pltpu.VMEM((2, 16, far_rows, width), jnp.bfloat16),
            pltpu.VMEM((2, 16, near_rows, width), jnp.bfloat16),
            pltpu.VMEM((2, 16, far_rows, width), jnp.bfloat16),
            pltpu.VMEM((width, both), jnp.bfloat16),
            pltpu.VMEM((rows, both // 2), jnp.bfloat16),
            pltpu.SemaphoreType.DMA((16,)),
        ],
        compiler_params=pltpu.CompilerParams(vmem_limit_bytes=60 << 20),
        cost_estimate=pl.CostEstimate(
            flops=3 * rows * both * width, bytes_accessed=width * both * 2 + rows * width * 4, transcendentals=rows * both // 2
        ),
    )(starts, *near, *far, *blocks)


def pack_kernel(flag_ref, core_ref, gate_ref, up_ref, other_gate_ref, other_up_ref, mine_ref, theirs_ref):
    swapped = flag_ref[0] == 1
    units = gate_ref.shape[1]
    unit = lax.broadcasted_iota(jnp.int32, (units, units // 2), 0)
    column = lax.broadcasted_iota(jnp.int32, (units, units // 2), 1)
    for target, core in ((mine_ref, core_ref[0]), (theirs_ref, 1 - core_ref[0])):
        chosen = (unit == (column // 96 * 2 + core) * 96 + column % 96).astype(jnp.bfloat16)
        for at, here, there in ((0, gate_ref, other_gate_ref), (1, up_ref, other_up_ref)):
            held = jnp.where(swapped, there[...], here[...])
            target[:, at * units // 2 : (at + 1) * units // 2] = jnp.dot(
                held, chosen, preferred_element_type=jnp.float32
            ).astype(jnp.bfloat16)


def pack(flag, core, *matrices):
    smem, vmem = pl.BlockSpec(memory_space=pltpu.SMEM), pl.BlockSpec(memory_space=pltpu.VMEM)
    shape = jax.ShapeDtypeStruct(matrices[0].shape, jnp.bfloat16)
    return pl.pallas_call(
        pack_kernel, in_specs=[smem] * 2 + [vmem] * 4, out_specs=[vmem] * 2, out_shape=[shape] * 2
    )(flag, core, *matrices)


def together(*values):
    return lax.optimization_barrier(values)


def z_steps(step_of):
    pairs = []
    for line in range(4):
        to, by = step_of[line]
        pairs += [(line * 4 + hi, to * 4 + (hi + by) % 4) for hi in range(4)]
    return pairs


def shards(tokens, cotangent, w_gate, w_up, expert_ids, gate_num, swap_flags):
    tok_count, width = tokens.shape
    deep = w_gate.shape[1]
    ahead, back = [(i, (i + 1) % 4) for i in range(4)], [(i, (i - 1) % 4) for i in range(4)]
    opposite = [(i, (i + 2) % 4) for i in range(4)]
    cores = [(0, 1), (1, 0)]
    along_z = ("zl", "zh")
    first = z_steps([(0, 1), (2, -1), (1, 1), (3, -1)])
    second = z_steps([(2, -1), (0, 1), (3, -1), (1, 1)])
    onward = z_steps([(0, 1), (1, 1), (2, -1), (3, -1)])
    place, line, core = lax.axis_index("zh"), lax.axis_index("zl"), lax.axis_index("c")
    me = (lax.axis_index("x") * 4 + place) * 4 + lax.axis_index("y")
    select = functools.partial(route, swap_flags, place.reshape(1), width)
    meta = jnp.concatenate([expert_ids, gate_num], axis=1).astype(jnp.bfloat16)
    meta = jnp.pad(meta, ((0, tok_count), (0, 128 - meta.shape[1])))
    own = jnp.concatenate([jnp.concatenate([tokens, cotangent], axis=0), meta], axis=1)
    rows_a, rows_b = lax.ppermute(own, along_z, first), lax.ppermute(own, along_z, second)
    flag = lax.dynamic_slice(swap_flags, (me % 32,), (1,))
    mine, theirs = pack(
        flag,
        core.reshape(1),
        w_gate[0],
        w_up[0],
        lax.ppermute(w_gate[0], "x", opposite),
        lax.ppermute(w_up[0], "x", opposite),
    )
    block = jnp.concatenate([mine, lax.ppermute(theirs, "c", cores)], axis=0)
    near_send, rows_a, block, block_l = together(
        select([(own, own), (rows_a, rows_a), (rows_b, rows_b)]), rows_a, block, lax.ppermute(block, "zl", ahead)
    )
    rows_f = lax.ppermute(rows_a, along_z, onward)
    near, far_send, block_r, block_fl = together(
        lax.all_to_all(near_send, PLANE, 0, 0, tiled=True),
        select([(rows_f, rows_f)]),
        lax.ppermute(block, "zl", back),
        lax.ppermute(block_l[:deep], "zl", ahead),
    )
    far, block_fr, near_c = together(
        lax.all_to_all(far_send, PLANE, 0, 0, tiled=True),
        lax.ppermute(block_r[deep:], "zl", back),
        lax.ppermute(near, "c", cores),
    )
    far_c = lax.ppermute(far, "c", cores)
    away = jnp.array([0, 0, 3, 3, 1, 1, 2, 2], jnp.int32)
    which = jnp.array([0, 1, 0, 1, 0, 1, 0, 1], jnp.int32)
    starts = (2 * ((line + away) % 4) + (core + which) % 2) * deep
    partial = compute(starts, [near, near_c], [far, far_c], [block, block_l, block_r, block_fl, block_fr])
    return lax.psum_scatter(partial, "zl", scatter_dimension=0, tiled=True).astype(jnp.float32)[None]


def solution(mesh):
    fine = Mesh(mesh.devices.reshape(4, 2, 4, 4, 4), ("zl", "c", "x", "zh", "y"))
    rows = P(("zl", "c", "x", "zh", "y"), None)
    split = P(("x", "zh", "y"), ("zl", "c"), None)
    in_specs = (rows, rows, split, split, rows, rows, P())
    return jax.shard_map(shards, mesh=fine, in_specs=in_specs, out_specs=split, check_vma=False)
```

```python
import functools

import jax
import jax.numpy as jnp
from jax import lax
from jax.experimental import pallas as pl
from jax.experimental.pallas import tpu as pltpu
from jax.sharding import Mesh, PartitionSpec as P

PLANE = ("x", "y")
RANKS = 8


def route_kernel(count, flags_ref, place_ref, *refs):
    metas, xs, ys = refs[:count], refs[count : 2 * count], refs[2 * count : 3 * count]
    out_ref, pick_ref, weigh_ref = refs[3 * count :]
    tok_count = metas[0].shape[0]
    slots = pick_ref.shape[2]

    @pl.when(pl.program_id(0) == 0)
    def _():
        lane = lax.broadcasted_iota(jnp.int32, (1, slots), 1)
        expert = jnp.zeros((1, slots), jnp.int32)
        for j in range(16):
            home = (j // 4) * 16 + place_ref[0] * 4 + j % 4
            other = lax.rem(home + 32, 64)
            held = jnp.where(flags_ref[lax.rem(home, 32)] == 1, other, home)
            expert = jnp.where(lane // RANKS == j, held, expert)
        expert = expert.astype(jnp.float32)
        rank_of = (lane % RANKS).astype(jnp.float32)
        earlier = (
            lax.broadcasted_iota(jnp.int32, (tok_count, tok_count), 0)
            > lax.broadcasted_iota(jnp.int32, (tok_count, tok_count), 1)
        ).astype(jnp.bfloat16)
        for s in range(count):
            meta = metas[s][...].astype(jnp.float32)
            weight = jnp.zeros((tok_count, slots), jnp.float32)
            for k in range(6):
                weight = jnp.where(meta[:, k : k + 1] == expert, meta[:, 6 + k : 7 + k], weight)
            chosen = jnp.where(weight > 0.0, 1.0, 0.0)
            before = jnp.dot(earlier, chosen.astype(jnp.bfloat16), preferred_element_type=jnp.float32)
            here = before == rank_of
            pick_ref[s] = jnp.where(here, chosen, 0.0).astype(jnp.bfloat16)
            weigh_ref[s] = jnp.where(here, weight * (1.0 / 64.0), 0.0).astype(jnp.bfloat16)

    for base, picks, rows in ((0, pick_ref, xs), (count, weigh_ref, ys)):
        for s in range(count):
            picked = lax.dot_general(
                picks[s], rows[s][...], (((0,), (0,)), ((), ())), preferred_element_type=jnp.float32
            )
            at = (base + s) * RANKS
            out_ref[:, at : at + RANKS, :] = picked.reshape(16, RANKS, picked.shape[1]).astype(jnp.bfloat16)


def route(flags, place, width, sources):
    count = len(sources)
    tok_count = 64
    tile = 512
    meta_block = width // 128
    smem = pl.BlockSpec(memory_space=pltpu.SMEM)
    x_of, y_of = [pair[0] for pair in sources], [pair[1] for pair in sources]
    y_block = 1 if x_of[0] is y_of[0] else 0
    return pl.pallas_call(
        functools.partial(route_kernel, count),
        grid=(width // tile,),
        in_specs=[smem] * 2
        + [pl.BlockSpec((tok_count, 128), lambda i: (0, meta_block))] * count
        + [pl.BlockSpec((tok_count, tile), lambda i: (0, i))] * count
        + [pl.BlockSpec((tok_count, tile), lambda i: (y_block, i))] * count,
        out_specs=pl.BlockSpec((16, 2 * count * RANKS, tile), lambda i: (0, 0, i)),
        out_shape=jax.ShapeDtypeStruct((16, 2 * count * RANKS, width), jnp.bfloat16),
        scratch_shapes=[pltpu.VMEM((count, tok_count, 16 * RANKS), jnp.bfloat16)] * 2,
        cost_estimate=pl.CostEstimate(
            flops=40_000_000_000,
            bytes_accessed=2 * count * (tok_count + 128) * width * 2,
            transcendentals=0,
        ),
    )(flags, place, *x_of, *x_of, *y_of)


def gate_kernel(starts_ref, near, near_c, b0, b1, b2, b3, b4, full, hidden, x_rows, sem):
    half = x_rows.shape[2]
    blocks, copies = (b0, b1, b2, b3, b4), []

    def begin(source, target):
        copies.append(pltpu.make_async_copy(source, target, sem.at[len(copies)]))
        copies[-1].start()

    begin(near.at[:, :half, :], x_rows.at[0])
    begin(near_c.at[:, :half, :], x_rows.at[1])
    deep = b3.shape[0]
    for b in range(5):
        for part in range(blocks[b].shape[0] // deep):
            start = pl.multiple_of(starts_ref[(2 * b + part) if b < 3 else 3 + b], 16)
            begin(blocks[b].at[part * deep : (part + 1) * deep, :], full.at[pl.ds(start, deep), :])
    for copy in copies:
        copy.wait()
    gate_rows(x_rows, full, hidden)


def gate_rows(x_rows, full, hidden):
    total, units = hidden.shape
    x_all = x_rows.reshape(total, full.shape[0])
    tile = 256
    for m in range(total // tile):
        at = slice(m * tile, (m + 1) * tile)
        sums = jnp.dot(x_all[at, :], full[...], preferred_element_type=jnp.float32)
        hidden[at, :] = (jax.nn.silu(sums[:, :units]) * sums[:, units:]).astype(jnp.bfloat16)


def gate_near(starts, near, near_c, blocks):
    half, width = near.shape[1] // 2, near.shape[2]
    rows, both = 32 * half, blocks[0].shape[1]
    hbm, vmem = pl.BlockSpec(memory_space=pltpu.HBM), pl.BlockSpec(memory_space=pltpu.VMEM)
    return pl.pallas_call(
        gate_kernel,
        in_specs=[pl.BlockSpec(memory_space=pltpu.SMEM)] + [hbm] * 7,
        out_specs=[vmem] * 2,
        out_shape=[
            jax.ShapeDtypeStruct((width, both), jnp.bfloat16),
            jax.ShapeDtypeStruct((rows, both // 2), jnp.bfloat16),
        ],
        scratch_shapes=[pltpu.VMEM((2, 16, half, width), jnp.bfloat16), pltpu.SemaphoreType.DMA((10,))],
        compiler_params=pltpu.CompilerParams(vmem_limit_bytes=60 << 20),
        cost_estimate=pl.CostEstimate(
            flops=2 * rows * both * width, bytes_accessed=2 * width * both * 2 + rows * width * 2, transcendentals=rows * both // 2
        ),
    )(starts, near, near_c, *blocks)


def grad_kernel(line_ref, near, near_c, far, far_c, full, hidden_near, out_ref, y_near, x_far, y_far, hidden_far, sem):
    n_half, f_half = y_near.shape[2], x_far.shape[2]
    copies = []

    def begin(source, target):
        copies.append(pltpu.make_async_copy(source, target, sem.at[len(copies)]))
        copies[-1].start()

    for core, rows in enumerate((far, far_c)):
        begin(rows.at[:, :f_half, :], x_far.at[core])
    for core, rows in enumerate((far, far_c)):
        begin(rows.at[:, f_half:, :], y_far.at[core])
    for core, rows in enumerate((near, near_c)):
        begin(rows.at[:, n_half:, :], y_near.at[core])
    for copy in copies[:2]:
        copy.wait()
    gate_rows(x_far, full, hidden_far)
    for copy in copies[2:]:
        copy.wait()
    width = full.shape[0]
    y_n, y_f = y_near.reshape(hidden_near.shape[0], width), y_far.reshape(hidden_far.shape[0], width)
    over_rows = (((0,), (0,)), ((), ()))
    deep = out_ref.shape[1]
    wide = 512
    for d in range(width // wide):
        cols = slice(d * wide, (d + 1) * wide)
        sums = lax.dot_general(hidden_near[...], y_n[:, cols], over_rows, preferred_element_type=jnp.float32)
        sums += lax.dot_general(hidden_far[...], y_f[:, cols], over_rows, preferred_element_type=jnp.float32)
        for owner in range(4):
            at = lax.rem(owner - line_ref[0] + 4, 4)
            out_ref[at, :, cols] = sums[owner * deep : (owner + 1) * deep, :].astype(jnp.bfloat16)


def gradients(line, near, near_c, far, far_c, full, hidden_near):
    n_half, f_half, width = near.shape[1] // 2, far.shape[1] // 2, near.shape[2]
    units = hidden_near.shape[1]
    rows = 32 * (n_half + f_half)
    hbm, vmem = pl.BlockSpec(memory_space=pltpu.HBM), pl.BlockSpec(memory_space=pltpu.VMEM)
    return pl.pallas_call(
        grad_kernel,
        in_specs=[pl.BlockSpec(memory_space=pltpu.SMEM)] + [hbm] * 4 + [vmem] * 2,
        out_specs=vmem,
        out_shape=jax.ShapeDtypeStruct((4, units // 4, width), jnp.bfloat16),
        scratch_shapes=[
            pltpu.VMEM((2, 16, n_half, width), jnp.bfloat16),
            pltpu.VMEM((2, 16, f_half, width), jnp.bfloat16),
            pltpu.VMEM((2, 16, f_half, width), jnp.bfloat16),
            pltpu.VMEM((32 * f_half, units), jnp.bfloat16),
            pltpu.SemaphoreType.DMA((6,)),
        ],
        compiler_params=pltpu.CompilerParams(vmem_limit_bytes=60 << 20),
        cost_estimate=pl.CostEstimate(
            flops=2 * rows * units * width + 128 * f_half * units * width,
            bytes_accessed=2 * width * units * 2 + rows * width * 2,
            transcendentals=32 * f_half * units,
        ),
    )(line, near, near_c, far, far_c, full, hidden_near)


def pack_kernel(flag_ref, core_ref, gate_ref, up_ref, other_gate_ref, other_up_ref, mine_ref, theirs_ref):
    swapped = flag_ref[0] == 1
    units = gate_ref.shape[1]
    unit = lax.broadcasted_iota(jnp.int32, (units, units // 2), 0)
    column = lax.broadcasted_iota(jnp.int32, (units, units // 2), 1)
    for target, core in ((mine_ref, core_ref[0]), (theirs_ref, 1 - core_ref[0])):
        chosen = (unit == (column // 96 * 2 + core) * 96 + column % 96).astype(jnp.bfloat16)
        for at, here, there in ((0, gate_ref, other_gate_ref), (1, up_ref, other_up_ref)):
            held = jnp.where(swapped, there[...], here[...])
            target[:, at * units // 2 : (at + 1) * units // 2] = jnp.dot(
                held, chosen, preferred_element_type=jnp.float32
            ).astype(jnp.bfloat16)


def pack(flag, core, *matrices):
    smem, vmem = pl.BlockSpec(memory_space=pltpu.SMEM), pl.BlockSpec(memory_space=pltpu.VMEM)
    shape = jax.ShapeDtypeStruct(matrices[0].shape, jnp.bfloat16)
    return pl.pallas_call(
        pack_kernel, in_specs=[smem] * 2 + [vmem] * 4, out_specs=[vmem] * 2, out_shape=[shape] * 2
    )(flag, core, *matrices)


def together(*values):
    return lax.optimization_barrier(values)


def z_steps(step_of):
    pairs = []
    for line in range(4):
        to, by = step_of[line]
        pairs += [(line * 4 + hi, to * 4 + (hi + by) % 4) for hi in range(4)]
    return pairs


def shards(tokens, cotangent, w_gate, w_up, expert_ids, gate_num, swap_flags):
    tok_count, width = tokens.shape
    deep = w_gate.shape[1]
    ahead, back = [(i, (i + 1) % 4) for i in range(4)], [(i, (i - 1) % 4) for i in range(4)]
    opposite = [(i, (i + 2) % 4) for i in range(4)]
    cores = [(0, 1), (1, 0)]
    along_z = ("zl", "zh")
    first = z_steps([(0, 1), (2, -1), (1, 1), (3, -1)])
    second = z_steps([(2, -1), (0, 1), (3, -1), (1, 1)])
    onward = z_steps([(0, 1), (1, 1), (2, -1), (3, -1)])
    place, line, core = lax.axis_index("zh"), lax.axis_index("zl"), lax.axis_index("c")
    me = (lax.axis_index("x") * 4 + place) * 4 + lax.axis_index("y")
    select = functools.partial(route, swap_flags, place.reshape(1), width)
    meta = jnp.concatenate([expert_ids, gate_num], axis=1).astype(jnp.bfloat16)
    meta = jnp.pad(meta, ((0, tok_count), (0, 128 - meta.shape[1])))
    own = jnp.concatenate([jnp.concatenate([tokens, cotangent], axis=0), meta], axis=1)
    rows_a, rows_b = lax.ppermute(own, along_z, first), lax.ppermute(own, along_z, second)
    flag = lax.dynamic_slice(swap_flags, (me % 32,), (1,))
    mine, theirs = pack(
        flag,
        core.reshape(1),
        w_gate[0],
        w_up[0],
        lax.ppermute(w_gate[0], "x", opposite),
        lax.ppermute(w_up[0], "x", opposite),
    )
    block = jnp.concatenate([mine, lax.ppermute(theirs, "c", cores)], axis=0)
    near_send, rows_a = together(select([(own, own), (rows_a, rows_a), (rows_b, rows_b)]), rows_a)
    rows_f = lax.ppermute(rows_a, along_z, onward)
    block_l, block_r = lax.ppermute(block, "zl", ahead), lax.ppermute(block, "zl", back)
    near, far_send, block_l, block_r, block_fl, block_fr = together(
        lax.all_to_all(near_send, PLANE, 0, 0, tiled=True),
        select([(rows_f, rows_f)]),
        block_l,
        block_r,
        lax.ppermute(block_l[:deep], "zl", ahead),
        lax.ppermute(block_r[deep:], "zl", back),
    )
    far = lax.all_to_all(far_send, PLANE, 0, 0, tiled=True)
    near_c = lax.ppermute(near, "c", cores)
    away = jnp.array([0, 0, 3, 3, 1, 1, 2, 2], jnp.int32)
    which = jnp.array([0, 1, 0, 1, 0, 1, 0, 1], jnp.int32)
    starts = (2 * ((line + away) % 4) + (core + which) % 2) * deep
    full, hidden = gate_near(starts, near, near_c, [block, block_l, block_r, block_fl, block_fr])
    far, full, hidden = together(far, full, hidden)
    far_c = lax.ppermute(far, "c", cores)
    partial = gradients(line.reshape(1), near, near_c, far, far_c, full, hidden)
    total = partial[0].astype(jnp.float32)
    for s in (2, 1, 3):
        total += lax.ppermute(partial[s], "zl", [(i, (i + s) % 4) for i in range(4)]).astype(jnp.float32)
    return total[None]


def solution(mesh):
    fine = Mesh(mesh.devices.reshape(4, 2, 4, 4, 4), ("zl", "c", "x", "zh", "y"))
    rows = P(("zl", "c", "x", "zh", "y"), None)
    split = P(("x", "zh", "y"), ("zl", "c"), None)
    in_specs = (rows, rows, split, split, rows, rows, P())
    return jax.shard_map(shards, mesh=fine, in_specs=in_specs, out_specs=split, check_vma=False)
```

```python
import functools

import jax
import jax.numpy as jnp
from jax import lax
from jax.experimental import pallas as pl
from jax.experimental.pallas import tpu as pltpu
from jax.sharding import Mesh, PartitionSpec as P

PLANE = ("x", "y")
RANKS = 8


def route_kernel(count, flags_ref, place_ref, *refs):
    metas, xs, ys = refs[:count], refs[count : 2 * count], refs[2 * count : 3 * count]
    out_ref, pick_ref, weigh_ref = refs[3 * count :]
    tok_count = metas[0].shape[0]
    slots = pick_ref.shape[2]

    @pl.when(pl.program_id(0) == 0)
    def _():
        lane = lax.broadcasted_iota(jnp.int32, (1, slots), 1)
        expert = jnp.zeros((1, slots), jnp.int32)
        for j in range(16):
            home = (j // 4) * 16 + place_ref[0] * 4 + j % 4
            other = lax.rem(home + 32, 64)
            held = jnp.where(flags_ref[lax.rem(home, 32)] == 1, other, home)
            expert = jnp.where(lane // RANKS == j, held, expert)
        expert = expert.astype(jnp.float32)
        rank_of = (lane % RANKS).astype(jnp.float32)
        earlier = (
            lax.broadcasted_iota(jnp.int32, (tok_count, tok_count), 0)
            > lax.broadcasted_iota(jnp.int32, (tok_count, tok_count), 1)
        ).astype(jnp.bfloat16)
        for s in range(count):
            meta = metas[s][...].astype(jnp.float32)
            weight = jnp.zeros((tok_count, slots), jnp.float32)
            for k in range(6):
                weight = jnp.where(meta[:, k : k + 1] == expert, meta[:, 6 + k : 7 + k], weight)
            chosen = jnp.where(weight > 0.0, 1.0, 0.0)
            before = jnp.dot(earlier, chosen.astype(jnp.bfloat16), preferred_element_type=jnp.float32)
            here = before == rank_of
            pick_ref[s] = jnp.where(here, chosen, 0.0).astype(jnp.bfloat16)
            weigh_ref[s] = jnp.where(here, weight * (1.0 / 64.0), 0.0).astype(jnp.bfloat16)

    for base, picks, rows in ((0, pick_ref, xs), (count, weigh_ref, ys)):
        for s in range(count):
            picked = lax.dot_general(
                picks[s], rows[s][...], (((0,), (0,)), ((), ())), preferred_element_type=jnp.float32
            )
            at = (base + s) * RANKS
            out_ref[:, at : at + RANKS, :] = picked.reshape(16, RANKS, picked.shape[1]).astype(jnp.bfloat16)


def route(flags, place, width, sources):
    count = len(sources)
    tok_count = 64
    tile = 512
    meta_block = width // 128
    smem = pl.BlockSpec(memory_space=pltpu.SMEM)
    x_of, y_of = [pair[0] for pair in sources], [pair[1] for pair in sources]
    y_block = 1 if x_of[0] is y_of[0] else 0
    return pl.pallas_call(
        functools.partial(route_kernel, count),
        grid=(width // tile,),
        in_specs=[smem] * 2
        + [pl.BlockSpec((tok_count, 128), lambda i: (0, meta_block))] * count
        + [pl.BlockSpec((tok_count, tile), lambda i: (0, i))] * count
        + [pl.BlockSpec((tok_count, tile), lambda i: (y_block, i))] * count,
        out_specs=pl.BlockSpec((16, 2 * count * RANKS, tile), lambda i: (0, 0, i)),
        out_shape=jax.ShapeDtypeStruct((16, 2 * count * RANKS, width), jnp.bfloat16),
        scratch_shapes=[pltpu.VMEM((count, tok_count, 16 * RANKS), jnp.bfloat16)] * 2,
        cost_estimate=pl.CostEstimate(
            flops=40_000_000_000,
            bytes_accessed=2 * count * (tok_count + 128) * width * 2,
            transcendentals=0,
        ),
    )(flags, place, *x_of, *x_of, *y_of)


def gate_rows(x_rows, full, hidden):
    total, units = hidden.shape
    x_all = x_rows.reshape(total, full.shape[0])
    tile = 256
    for m in range(total // tile):
        at = slice(m * tile, (m + 1) * tile)
        sums = jnp.dot(x_all[at, :], full[...], preferred_element_type=jnp.float32)
        hidden[at, :] = (jax.nn.silu(sums[:, :units]) * sums[:, units:]).astype(jnp.bfloat16)


def over_rows(hidden, y_rows, cols):
    return lax.dot_general(
        hidden[...], y_rows[:, cols], (((0,), (0,)), ((), ())), preferred_element_type=jnp.float32
    )


def starter(sem):
    copies = []

    def begin(source, target):
        copies.append(pltpu.make_async_copy(source, target, sem.at[len(copies)]))
        copies[-1].start()

    return copies, begin


WIDE = 512


def near_kernel(starts_ref, near, near_c, b0, b1, b2, b3, b4, b5, full, sums_ref, x_rows, y_rows, hidden, sem):
    half = x_rows.shape[2]
    copies, begin = starter(sem)
    begin(near.at[:, :half, :], x_rows.at[0])
    begin(near_c.at[:, :half, :], x_rows.at[1])
    deep = b3.shape[0]
    pieces = [(block.at[part * deep : (part + 1) * deep, :], 0) for block in (b0, b1, b2) for part in range(2)]
    pieces += [(b3, 0), (b4, 0), (b5, b4.shape[0])]
    for p, (piece, past) in enumerate(pieces):
        start = pl.multiple_of(starts_ref[min(p, 7)] + past, 16)
        begin(piece, full.at[pl.ds(start, piece.shape[0]), :])
    begin(near.at[:, half:, :], y_rows.at[0])
    begin(near_c.at[:, half:, :], y_rows.at[1])
    for copy in copies[:-2]:
        copy.wait()
    gate_rows(x_rows, full, hidden)
    for copy in copies[-2:]:
        copy.wait()
    y_all = y_rows.reshape(hidden.shape[0], full.shape[0])
    for d in range(full.shape[0] // WIDE):
        cols = slice(d * WIDE, (d + 1) * WIDE)
        sums_ref[:, cols] = over_rows(hidden, y_all, cols)


def near_sums(starts, near, near_c, blocks):
    half, width = near.shape[1] // 2, near.shape[2]
    rows, both = 32 * half, blocks[0].shape[1]
    hbm, vmem = pl.BlockSpec(memory_space=pltpu.HBM), pl.BlockSpec(memory_space=pltpu.VMEM)
    return pl.pallas_call(
        near_kernel,
        in_specs=[pl.BlockSpec(memory_space=pltpu.SMEM)] + [hbm] * 8,
        out_specs=[vmem] * 2,
        out_shape=[
            jax.ShapeDtypeStruct((width, both), jnp.bfloat16),
            jax.ShapeDtypeStruct((both // 2, width), jnp.float32),
        ],
        scratch_shapes=[
            pltpu.VMEM((2, 16, half, width), jnp.bfloat16),
            pltpu.VMEM((2, 16, half, width), jnp.bfloat16),
            pltpu.VMEM((rows, both // 2), jnp.bfloat16),
            pltpu.SemaphoreType.DMA((13,)),
        ],
        compiler_params=pltpu.CompilerParams(vmem_limit_bytes=60 << 20),
        cost_estimate=pl.CostEstimate(
            flops=3 * rows * both * width, bytes_accessed=4 * width * both * 2 + rows * width * 4, transcendentals=rows * both // 2
        ),
    )(starts, near, near_c, *blocks)


def far_kernel(line_ref, far, far_c, full_hbm, sums_hbm, *refs):
    outs = refs[:4]
    x_rows, y_rows, full, sums, hidden, sem = refs[4:]
    half = x_rows.shape[2]
    copies, begin = starter(sem)
    begin(full_hbm, full)
    for core, rows in enumerate((far, far_c)):
        begin(rows.at[:, :half, :], x_rows.at[core])
    for core, rows in enumerate((far, far_c)):
        begin(rows.at[:, half:, :], y_rows.at[core])
    begin(sums_hbm, sums)
    for copy in copies[:3]:
        copy.wait()
    gate_rows(x_rows, full, hidden)
    for copy in copies[3:]:
        copy.wait()
    y_all = y_rows.reshape(hidden.shape[0], full.shape[0])
    deep = outs[0].shape[0]
    for d in range(full.shape[0] // WIDE):
        cols = slice(d * WIDE, (d + 1) * WIDE)
        done = (sums[:, cols] + over_rows(hidden, y_all, cols)).astype(jnp.bfloat16)
        for line in range(4):

            @pl.when(line_ref[0] == line)
            def _(line=line, cols=cols, done=done):
                for s in range(4):
                    owner = (line + s) % 4
                    outs[s][:, cols] = done[owner * deep : (owner + 1) * deep, :]


def chunks(line, far, far_c, full, sums):
    half, width = far.shape[1] // 2, far.shape[2]
    units, rows = sums.shape[0], 32 * half
    hbm, vmem = pl.BlockSpec(memory_space=pltpu.HBM), pl.BlockSpec(memory_space=pltpu.VMEM)
    return pl.pallas_call(
        far_kernel,
        in_specs=[pl.BlockSpec(memory_space=pltpu.SMEM)] + [hbm] * 4,
        out_specs=[vmem] * 4,
        out_shape=[jax.ShapeDtypeStruct((units // 4, width), jnp.bfloat16)] * 4,
        scratch_shapes=[
            pltpu.VMEM((2, 16, half, width), jnp.bfloat16),
            pltpu.VMEM((2, 16, half, width), jnp.bfloat16),
            pltpu.VMEM(full.shape, jnp.bfloat16),
            pltpu.VMEM(sums.shape, jnp.float32),
            pltpu.VMEM((rows, units), jnp.bfloat16),
            pltpu.SemaphoreType.DMA((6,)),
        ],
        compiler_params=pltpu.CompilerParams(vmem_limit_bytes=60 << 20),
        cost_estimate=pl.CostEstimate(
            flops=6 * rows * units * width, bytes_accessed=10 * width * units + rows * width * 4, transcendentals=rows * units
        ),
    )(line, far, far_c, full, sums)


def pack_kernel(flag_ref, core_ref, gate_ref, up_ref, other_gate_ref, other_up_ref, mine_ref, theirs_ref):
    swapped = flag_ref[0] == 1
    units = gate_ref.shape[1]
    unit = lax.broadcasted_iota(jnp.int32, (units, units // 2), 0)
    column = lax.broadcasted_iota(jnp.int32, (units, units // 2), 1)
    for target, core in ((mine_ref, core_ref[0]), (theirs_ref, 1 - core_ref[0])):
        chosen = (unit == (column // 96 * 2 + core) * 96 + column % 96).astype(jnp.bfloat16)
        for at, here, there in ((0, gate_ref, other_gate_ref), (1, up_ref, other_up_ref)):
            held = jnp.where(swapped, there[...], here[...])
            target[:, at * units // 2 : (at + 1) * units // 2] = jnp.dot(
                held, chosen, preferred_element_type=jnp.float32
            ).astype(jnp.bfloat16)


def pack(flag, core, *matrices):
    smem, vmem = pl.BlockSpec(memory_space=pltpu.SMEM), pl.BlockSpec(memory_space=pltpu.VMEM)
    shape = jax.ShapeDtypeStruct(matrices[0].shape, jnp.bfloat16)
    return pl.pallas_call(
        pack_kernel, in_specs=[smem] * 2 + [vmem] * 4, out_specs=[vmem] * 2, out_shape=[shape] * 2
    )(flag, core, *matrices)


def together(*values):
    return lax.optimization_barrier(values)


def z_steps(step_of):
    pairs = []
    for line in range(4):
        to, by = step_of[line]
        pairs += [(line * 4 + hi, to * 4 + (hi + by) % 4) for hi in range(4)]
    return pairs


def shards(tokens, cotangent, w_gate, w_up, expert_ids, gate_num, swap_flags):
    tok_count, width = tokens.shape
    deep = w_gate.shape[1]
    ahead, back = [(i, (i + 1) % 4) for i in range(4)], [(i, (i - 1) % 4) for i in range(4)]
    opposite = [(i, (i + 2) % 4) for i in range(4)]
    cores = [(0, 1), (1, 0)]
    along_z = ("zl", "zh")
    first = z_steps([(0, 1), (2, -1), (1, 1), (3, -1)])
    second = z_steps([(2, -1), (0, 1), (3, -1), (1, 1)])
    onward = z_steps([(0, 1), (1, 1), (2, -1), (3, -1)])
    place, line, core = lax.axis_index("zh"), lax.axis_index("zl"), lax.axis_index("c")
    me = (lax.axis_index("x") * 4 + place) * 4 + lax.axis_index("y")
    select = functools.partial(route, swap_flags, place.reshape(1), width)
    meta = jnp.concatenate([expert_ids, gate_num], axis=1).astype(jnp.bfloat16)
    meta = jnp.pad(meta, ((0, tok_count), (0, 128 - meta.shape[1])))
    own = jnp.concatenate([jnp.concatenate([tokens, cotangent], axis=0), meta], axis=1)
    rows_a, rows_b = lax.ppermute(own, along_z, first), lax.ppermute(own, along_z, second)
    flag = lax.dynamic_slice(swap_flags, (me % 32,), (1,))
    mine, theirs = pack(
        flag,
        core.reshape(1),
        w_gate[0],
        w_up[0],
        lax.ppermute(w_gate[0], "x", opposite),
        lax.ppermute(w_up[0], "x", opposite),
    )
    block = jnp.concatenate([mine, lax.ppermute(theirs, "c", cores)], axis=0)
    near_send, rows_a = together(select([(own, own), (rows_a, rows_a), (rows_b, rows_b)]), rows_a)
    rows_f = lax.ppermute(rows_a, along_z, onward)
    block_l, block_r = lax.ppermute(block, "zl", ahead), lax.ppermute(block, "zl", back)
    early = deep + deep // 4
    near, far_send, block_l, block_r, block_fl, block_fr = together(
        lax.all_to_all(near_send, PLANE, 0, 0, tiled=True),
        select([(rows_f, rows_f)]),
        block_l,
        block_r,
        lax.ppermute(block_l[:deep], "zl", ahead),
        lax.ppermute(block_r[deep:early], "zl", back),
    )
    rest_fr = lax.ppermute(block_r[early:], "zl", back)
    far = lax.all_to_all(far_send, PLANE, 0, 0, tiled=True)
    near_c = lax.ppermute(near, "c", cores)
    away = jnp.array([0, 0, 3, 3, 1, 1, 2, 2], jnp.int32)
    which = jnp.array([0, 1, 0, 1, 0, 1, 0, 1], jnp.int32)
    starts = (2 * ((line + away) % 4) + (core + which) % 2) * deep
    full, sums = near_sums(starts, near, near_c, [block, block_l, block_r, block_fl, block_fr, rest_fr])
    far, full, sums = together(far, full, sums)
    far_c = lax.ppermute(far, "c", cores)
    parts = chunks(line.reshape(1), far, far_c, full, sums)
    total = parts[0].astype(jnp.float32)
    for s in (2, 1, 3):
        total += lax.ppermute(parts[s], "zl", [(i, (i + s) % 4) for i in range(4)]).astype(jnp.float32)
    return total[None]


def solution(mesh):
    fine = Mesh(mesh.devices.reshape(4, 2, 4, 4, 4), ("zl", "c", "x", "zh", "y"))
    rows = P(("zl", "c", "x", "zh", "y"), None)
    split = P(("x", "zh", "y"), ("zl", "c"), None)
    in_specs = (rows, rows, split, split, rows, rows, P())
    return jax.shard_map(shards, mesh=fine, in_specs=in_specs, out_specs=split, check_vma=False)
```

```python
import functools

import jax
import jax.numpy as jnp
from jax import lax
from jax.experimental import pallas as pl
from jax.experimental.pallas import tpu as pltpu
from jax.sharding import Mesh, PartitionSpec as P

PLANE = ("x", "y")
RANKS = 8


def route_kernel(count, flags_ref, place_ref, *refs):
    metas, xs, ys = refs[:count], refs[count : 2 * count], refs[2 * count : 3 * count]
    out_ref, pick_ref, weigh_ref = refs[3 * count :]
    tok_count = metas[0].shape[0]
    slots = pick_ref.shape[2]

    @pl.when(pl.program_id(0) == 0)
    def _():
        lane = lax.broadcasted_iota(jnp.int32, (1, slots), 1)
        expert = jnp.zeros((1, slots), jnp.int32)
        for j in range(16):
            home = (j // 4) * 16 + place_ref[0] * 4 + j % 4
            other = lax.rem(home + 32, 64)
            held = jnp.where(flags_ref[lax.rem(home, 32)] == 1, other, home)
            expert = jnp.where(lane // RANKS == j, held, expert)
        expert = expert.astype(jnp.float32)
        rank_of = (lane % RANKS).astype(jnp.float32)
        earlier = (
            lax.broadcasted_iota(jnp.int32, (tok_count, tok_count), 0)
            > lax.broadcasted_iota(jnp.int32, (tok_count, tok_count), 1)
        ).astype(jnp.bfloat16)
        for s in range(count):
            meta = metas[s][...].astype(jnp.float32)
            weight = jnp.zeros((tok_count, slots), jnp.float32)
            for k in range(6):
                weight = jnp.where(meta[:, k : k + 1] == expert, meta[:, 6 + k : 7 + k], weight)
            chosen = jnp.where(weight > 0.0, 1.0, 0.0)
            before = jnp.dot(earlier, chosen.astype(jnp.bfloat16), preferred_element_type=jnp.float32)
            here = before == rank_of
            pick_ref[s] = jnp.where(here, chosen, 0.0).astype(jnp.bfloat16)
            weigh_ref[s] = jnp.where(here, weight * (1.0 / 64.0), 0.0).astype(jnp.bfloat16)

    for base, picks, rows in ((0, pick_ref, xs), (count, weigh_ref, ys)):
        for s in range(count):
            picked = lax.dot_general(
                picks[s], rows[s][...], (((0,), (0,)), ((), ())), preferred_element_type=jnp.float32
            )
            at = (base + s) * RANKS
            out_ref[:, at : at + RANKS, :] = picked.reshape(16, RANKS, picked.shape[1]).astype(jnp.bfloat16)


def route(flags, place, width, sources):
    count = len(sources)
    tok_count = 64
    tile = 512
    meta_block = width // 128
    smem = pl.BlockSpec(memory_space=pltpu.SMEM)
    x_of, y_of = [pair[0] for pair in sources], [pair[1] for pair in sources]
    y_block = 1 if x_of[0] is y_of[0] else 0
    return pl.pallas_call(
        functools.partial(route_kernel, count),
        grid=(width // tile,),
        in_specs=[smem] * 2
        + [pl.BlockSpec((tok_count, 128), lambda i: (0, meta_block))] * count
        + [pl.BlockSpec((tok_count, tile), lambda i: (0, i))] * count
        + [pl.BlockSpec((tok_count, tile), lambda i: (y_block, i))] * count,
        out_specs=pl.BlockSpec((16, 2 * count * RANKS, tile), lambda i: (0, 0, i)),
        out_shape=jax.ShapeDtypeStruct((16, 2 * count * RANKS, width), jnp.bfloat16),
        scratch_shapes=[pltpu.VMEM((count, tok_count, 16 * RANKS), jnp.bfloat16)] * 2,
        cost_estimate=pl.CostEstimate(
            flops=40_000_000_000,
            bytes_accessed=2 * count * (tok_count + 128) * width * 2,
            transcendentals=0,
        ),
    )(flags, place, *x_of, *x_of, *y_of)


def gate_rows(x_rows, full, hidden):
    total, units = hidden.shape
    x_all = x_rows.reshape(total, full.shape[0])
    tile = 256
    for m in range(total // tile):
        at = slice(m * tile, (m + 1) * tile)
        sums = jnp.dot(x_all[at, :], full[...], preferred_element_type=jnp.float32)
        hidden[at, :] = (jax.nn.silu(sums[:, :units]) * sums[:, units:]).astype(jnp.bfloat16)


def over_rows(hidden, y_rows, cols):
    return lax.dot_general(
        hidden[...], y_rows[:, cols], (((0,), (0,)), ((), ())), preferred_element_type=jnp.float32
    )


def starter(sem):
    copies = []

    def begin(source, target):
        copies.append(pltpu.make_async_copy(source, target, sem.at[len(copies)]))
        copies[-1].start()

    return copies, begin


def assemble(begin, starts_ref, blocks, full):
    deep = blocks[3].shape[0]
    pieces = [block.at[part * deep : (part + 1) * deep, :] for block in blocks[:3] for part in range(2)]
    for p, piece in enumerate(pieces + list(blocks[3:])):
        begin(piece, full.at[pl.ds(pl.multiple_of(starts_ref[p], 16), deep), :])


WIDE = 512


def near_kernel(starts_ref, near, near_c, b0, b1, b2, b3, b4, sums_ref, x_rows, y_rows, full, hidden, sem):
    half = x_rows.shape[2]
    copies, begin = starter(sem)
    begin(near.at[:, :half, :], x_rows.at[0])
    begin(near_c.at[:, :half, :], x_rows.at[1])
    assemble(begin, starts_ref, (b0, b1, b2, b3, b4), full)
    begin(near.at[:, half:, :], y_rows.at[0])
    begin(near_c.at[:, half:, :], y_rows.at[1])
    for copy in copies[:-2]:
        copy.wait()
    gate_rows(x_rows, full, hidden)
    for copy in copies[-2:]:
        copy.wait()
    y_all = y_rows.reshape(hidden.shape[0], full.shape[0])
    for d in range(full.shape[0] // WIDE):
        cols = slice(d * WIDE, (d + 1) * WIDE)
        sums_ref[:, cols] = over_rows(hidden, y_all, cols)


def near_sums(starts, near, near_c, blocks):
    half, width = near.shape[1] // 2, near.shape[2]
    rows, both = 32 * half, blocks[0].shape[1]
    hbm, vmem = pl.BlockSpec(memory_space=pltpu.HBM), pl.BlockSpec(memory_space=pltpu.VMEM)
    return pl.pallas_call(
        near_kernel,
        in_specs=[pl.BlockSpec(memory_space=pltpu.SMEM)] + [hbm] * 7,
        out_specs=vmem,
        out_shape=jax.ShapeDtypeStruct((both // 2, width), jnp.float32),
        scratch_shapes=[
            pltpu.VMEM((2, 16, half, width), jnp.bfloat16),
            pltpu.VMEM((2, 16, half, width), jnp.bfloat16),
            pltpu.VMEM((width, both), jnp.bfloat16),
            pltpu.VMEM((rows, both // 2), jnp.bfloat16),
            pltpu.SemaphoreType.DMA((12,)),
        ],
        compiler_params=pltpu.CompilerParams(vmem_limit_bytes=60 << 20),
        cost_estimate=pl.CostEstimate(
            flops=3 * rows * both * width, bytes_accessed=2 * width * both * 2 + rows * width * 4, transcendentals=rows * both // 2
        ),
    )(starts, near, near_c, *blocks)


def far_kernel(starts_ref, line_ref, far, far_c, b0, b1, b2, b3, b4, sums_hbm, *refs):
    outs = refs[:4]
    x_rows, y_rows, full, sums, hidden, sem = refs[4:]
    half = x_rows.shape[2]
    copies, begin = starter(sem)
    for core, rows in enumerate((far, far_c)):
        begin(rows.at[:, :half, :], x_rows.at[core])
    assemble(begin, starts_ref, (b0, b1, b2, b3, b4), full)
    for core, rows in enumerate((far, far_c)):
        begin(rows.at[:, half:, :], y_rows.at[core])
    begin(sums_hbm, sums)
    for copy in copies[:-3]:
        copy.wait()
    gate_rows(x_rows, full, hidden)
    for copy in copies[-3:]:
        copy.wait()
    y_all = y_rows.reshape(hidden.shape[0], full.shape[0])
    deep = outs[0].shape[0]
    for d in range(full.shape[0] // WIDE):
        cols = slice(d * WIDE, (d + 1) * WIDE)
        done = (sums[:, cols] + over_rows(hidden, y_all, cols)).astype(jnp.bfloat16)
        for line in range(4):

            @pl.when(line_ref[0] == line)
            def _(line=line, cols=cols, done=done):
                for s in range(4):
                    owner = (line + s) % 4
                    outs[s][:, cols] = done[owner * deep : (owner + 1) * deep, :]


def chunks(starts, line, far, far_c, blocks, sums):
    half, width = far.shape[1] // 2, far.shape[2]
    units, rows = sums.shape[0], 32 * half
    smem = pl.BlockSpec(memory_space=pltpu.SMEM)
    hbm, vmem = pl.BlockSpec(memory_space=pltpu.HBM), pl.BlockSpec(memory_space=pltpu.VMEM)
    return pl.pallas_call(
        far_kernel,
        in_specs=[smem] * 2 + [hbm] * 8,
        out_specs=[vmem] * 4,
        out_shape=[jax.ShapeDtypeStruct((units // 4, width), jnp.bfloat16)] * 4,
        scratch_shapes=[
            pltpu.VMEM((2, 16, half, width), jnp.bfloat16),
            pltpu.VMEM((2, 16, half, width), jnp.bfloat16),
            pltpu.VMEM((width, 2 * units), jnp.bfloat16),
            pltpu.VMEM(sums.shape, jnp.float32),
            pltpu.VMEM((rows, units), jnp.bfloat16),
            pltpu.SemaphoreType.DMA((13,)),
        ],
        compiler_params=pltpu.CompilerParams(vmem_limit_bytes=60 << 20),
        cost_estimate=pl.CostEstimate(
            flops=6 * rows * units * width, bytes_accessed=10 * width * units + rows * width * 4, transcendentals=rows * units
        ),
    )(starts, line, far, far_c, *blocks, sums)


def pack_kernel(flag_ref, core_ref, gate_ref, up_ref, other_gate_ref, other_up_ref, mine_ref, theirs_ref):
    swapped = flag_ref[0] == 1
    units = gate_ref.shape[1]
    unit = lax.broadcasted_iota(jnp.int32, (units, units // 2), 0)
    column = lax.broadcasted_iota(jnp.int32, (units, units // 2), 1)
    for target, core in ((mine_ref, core_ref[0]), (theirs_ref, 1 - core_ref[0])):
        chosen = (unit == (column // 96 * 2 + core) * 96 + column % 96).astype(jnp.bfloat16)
        for at, here, there in ((0, gate_ref, other_gate_ref), (1, up_ref, other_up_ref)):
            held = jnp.where(swapped, there[...], here[...])
            target[:, at * units // 2 : (at + 1) * units // 2] = jnp.dot(
                held, chosen, preferred_element_type=jnp.float32
            ).astype(jnp.bfloat16)


def pack(flag, core, *matrices):
    smem, vmem = pl.BlockSpec(memory_space=pltpu.SMEM), pl.BlockSpec(memory_space=pltpu.VMEM)
    shape = jax.ShapeDtypeStruct(matrices[0].shape, jnp.bfloat16)
    return pl.pallas_call(
        pack_kernel, in_specs=[smem] * 2 + [vmem] * 4, out_specs=[vmem] * 2, out_shape=[shape] * 2
    )(flag, core, *matrices)


def together(*values):
    return lax.optimization_barrier(values)


def z_steps(step_of):
    pairs = []
    for line in range(4):
        to, by = step_of[line]
        pairs += [(line * 4 + hi, to * 4 + (hi + by) % 4) for hi in range(4)]
    return pairs


def shards(tokens, cotangent, w_gate, w_up, expert_ids, gate_num, swap_flags):
    tok_count, width = tokens.shape
    deep = w_gate.shape[1]
    ahead, back = [(i, (i + 1) % 4) for i in range(4)], [(i, (i - 1) % 4) for i in range(4)]
    opposite = [(i, (i + 2) % 4) for i in range(4)]
    cores = [(0, 1), (1, 0)]
    along_z = ("zl", "zh")
    first = z_steps([(0, 1), (2, -1), (1, 1), (3, -1)])
    second = z_steps([(2, -1), (0, 1), (3, -1), (1, 1)])
    onward = z_steps([(0, 1), (1, 1), (2, -1), (3, -1)])
    place, line, core = lax.axis_index("zh"), lax.axis_index("zl"), lax.axis_index("c")
    me = (lax.axis_index("x") * 4 + place) * 4 + lax.axis_index("y")
    select = functools.partial(route, swap_flags, place.reshape(1), width)
    meta = jnp.concatenate([expert_ids, gate_num], axis=1).astype(jnp.bfloat16)
    meta = jnp.pad(meta, ((0, tok_count), (0, 128 - meta.shape[1])))
    own = jnp.concatenate([jnp.concatenate([tokens, cotangent], axis=0), meta], axis=1)
    rows_a, rows_b = lax.ppermute(own, along_z, first), lax.ppermute(own, along_z, second)
    flag = lax.dynamic_slice(swap_flags, (me % 32,), (1,))
    mine, theirs = pack(
        flag,
        core.reshape(1),
        w_gate[0],
        w_up[0],
        lax.ppermute(w_gate[0], "x", opposite),
        lax.ppermute(w_up[0], "x", opposite),
    )
    block = jnp.concatenate([mine, lax.ppermute(theirs, "c", cores)], axis=0)
    near_send, rows_a = together(select([(own, own), (rows_a, rows_a), (rows_b, rows_b)]), rows_a)
    rows_f, block, block_l = together(
        lax.ppermute(rows_a, along_z, onward), block, lax.ppermute(block, "zl", ahead)
    )
    near, far_send, block_r, block_fl = together(
        lax.all_to_all(near_send, PLANE, 0, 0, tiled=True),
        select([(rows_f, rows_f)]),
        lax.ppermute(block, "zl", back),
        lax.ppermute(block_l[:deep], "zl", ahead),
    )
    block_fr = lax.ppermute(block_r[deep:], "zl", back)
    far = lax.all_to_all(far_send, PLANE, 0, 0, tiled=True)
    near_c = lax.ppermute(near, "c", cores)
    away = jnp.array([0, 0, 3, 3, 1, 1, 2, 2], jnp.int32)
    which = jnp.array([0, 1, 0, 1, 0, 1, 0, 1], jnp.int32)
    starts = (2 * ((line + away) % 4) + (core + which) % 2) * deep
    blocks = [block, block_l, block_r, block_fl, block_fr]
    sums = near_sums(starts, near, near_c, blocks)
    far, sums = together(far, sums)
    far_c = lax.ppermute(far, "c", cores)
    parts = chunks(starts, line.reshape(1), far, far_c, blocks, sums)
    total = parts[0].astype(jnp.float32)
    for s in (2, 1, 3):
        total += lax.ppermute(parts[s], "zl", [(i, (i + s) % 4) for i in range(4)]).astype(jnp.float32)
    return total[None]


def solution(mesh):
    fine = Mesh(mesh.devices.reshape(4, 2, 4, 4, 4), ("zl", "c", "x", "zh", "y"))
    rows = P(("zl", "c", "x", "zh", "y"), None)
    split = P(("x", "zh", "y"), ("zl", "c"), None)
    in_specs = (rows, rows, split, split, rows, rows, P())
    return jax.shard_map(shards, mesh=fine, in_specs=in_specs, out_specs=split, check_vma=False)
```

```python
import functools

import jax
import jax.numpy as jnp
from jax import lax
from jax.experimental import pallas as pl
from jax.experimental.pallas import tpu as pltpu
from jax.sharding import Mesh, PartitionSpec as P

PLANE = ("x", "y")
RANKS = 8


def route_kernel(count, flags_ref, place_ref, *refs):
    metas, xs, ys = refs[:count], refs[count : 2 * count], refs[2 * count : 3 * count]
    out_ref, pick_ref, weigh_ref = refs[3 * count :]
    tok_count = metas[0].shape[0]
    slots = pick_ref.shape[2]

    @pl.when(pl.program_id(0) == 0)
    def _():
        lane = lax.broadcasted_iota(jnp.int32, (1, slots), 1)
        expert = jnp.zeros((1, slots), jnp.int32)
        for j in range(16):
            home = (j // 4) * 16 + place_ref[0] * 4 + j % 4
            other = lax.rem(home + 32, 64)
            held = jnp.where(flags_ref[lax.rem(home, 32)] == 1, other, home)
            expert = jnp.where(lane // RANKS == j, held, expert)
        expert = expert.astype(jnp.float32)
        rank_of = (lane % RANKS).astype(jnp.float32)
        earlier = (
            lax.broadcasted_iota(jnp.int32, (tok_count, tok_count), 0)
            > lax.broadcasted_iota(jnp.int32, (tok_count, tok_count), 1)
        ).astype(jnp.bfloat16)
        for s in range(count):
            meta = metas[s][...].astype(jnp.float32)
            weight = jnp.zeros((tok_count, slots), jnp.float32)
            for k in range(6):
                weight = jnp.where(meta[:, k : k + 1] == expert, meta[:, 6 + k : 7 + k], weight)
            chosen = jnp.where(weight > 0.0, 1.0, 0.0)
            before = jnp.dot(earlier, chosen.astype(jnp.bfloat16), preferred_element_type=jnp.float32)
            here = before == rank_of
            pick_ref[s] = jnp.where(here, chosen, 0.0).astype(jnp.bfloat16)
            weigh_ref[s] = jnp.where(here, weight * (1.0 / 64.0), 0.0).astype(jnp.bfloat16)

    for base, picks, rows in ((0, pick_ref, xs), (count, weigh_ref, ys)):
        for s in range(count):
            picked = lax.dot_general(
                picks[s], rows[s][...], (((0,), (0,)), ((), ())), preferred_element_type=jnp.float32
            )
            at = (base + s) * RANKS
            out_ref[:, at : at + RANKS, :] = picked.reshape(16, RANKS, picked.shape[1]).astype(jnp.bfloat16)


def route(flags, place, width, sources):
    count = len(sources)
    tok_count = 64
    tile = 512
    meta_block = width // 128
    smem = pl.BlockSpec(memory_space=pltpu.SMEM)
    x_of, y_of = [pair[0] for pair in sources], [pair[1] for pair in sources]
    y_block = 1 if x_of[0] is y_of[0] else 0
    return pl.pallas_call(
        functools.partial(route_kernel, count),
        grid=(width // tile,),
        in_specs=[smem] * 2
        + [pl.BlockSpec((tok_count, 128), lambda i: (0, meta_block))] * count
        + [pl.BlockSpec((tok_count, tile), lambda i: (0, i))] * count
        + [pl.BlockSpec((tok_count, tile), lambda i: (y_block, i))] * count,
        out_specs=pl.BlockSpec((16, 2 * count * RANKS, tile), lambda i: (0, 0, i)),
        out_shape=jax.ShapeDtypeStruct((16, 2 * count * RANKS, width), jnp.bfloat16),
        scratch_shapes=[pltpu.VMEM((count, tok_count, 16 * RANKS), jnp.bfloat16)] * 2,
        cost_estimate=pl.CostEstimate(
            flops=40_000_000_000,
            bytes_accessed=2 * count * (tok_count + 128) * width * 2,
            transcendentals=0,
        ),
    )(flags, place, *x_of, *x_of, *y_of)


def gate_rows(x_rows, full, hidden):
    total, units = hidden.shape
    x_all = x_rows.reshape(total, full.shape[0])
    tile = 256
    for m in range(total // tile):
        at = slice(m * tile, (m + 1) * tile)
        sums = jnp.dot(x_all[at, :], full[...], preferred_element_type=jnp.float32)
        hidden[at, :] = (jax.nn.silu(sums[:, :units]) * sums[:, units:]).astype(jnp.bfloat16)


def over_rows(hidden, y_rows, cols):
    return lax.dot_general(
        hidden[...], y_rows[:, cols], (((0,), (0,)), ((), ())), preferred_element_type=jnp.float32
    )


def starter(sem):
    copies = []

    def begin(source, target):
        copies.append(pltpu.make_async_copy(source, target, sem.at[len(copies)]))
        copies[-1].start()

    return copies, begin


WIDE = 512


def near_kernel(starts_ref, near, near_c, b0, b1, b2, b3, b4, b5, full, sums_ref, x_rows, y_rows, hidden, sem):
    half = x_rows.shape[2]
    copies, begin = starter(sem)
    begin(near.at[:, :half, :], x_rows.at[0])
    begin(near_c.at[:, :half, :], x_rows.at[1])
    deep = b3.shape[0]
    pieces = [(block.at[part * deep : (part + 1) * deep, :], 0) for block in (b0, b1, b2) for part in range(2)]
    pieces += [(b3, 0), (b4, 0), (b5, b4.shape[0])]
    for p, (piece, past) in enumerate(pieces):
        start = pl.multiple_of(starts_ref[min(p, 7)] + past, 16)
        begin(piece, full.at[pl.ds(start, piece.shape[0]), :])
    begin(near.at[:, half:, :], y_rows.at[0])
    begin(near_c.at[:, half:, :], y_rows.at[1])
    for copy in copies[:-2]:
        copy.wait()
    gate_rows(x_rows, full, hidden)
    for copy in copies[-2:]:
        copy.wait()
    y_all = y_rows.reshape(hidden.shape[0], full.shape[0])
    for d in range(full.shape[0] // WIDE):
        cols = slice(d * WIDE, (d + 1) * WIDE)
        sums_ref[:, cols] = over_rows(hidden, y_all, cols)


def near_sums(starts, near, near_c, blocks):
    half, width = near.shape[1] // 2, near.shape[2]
    rows, both = 32 * half, blocks[0].shape[1]
    hbm, vmem = pl.BlockSpec(memory_space=pltpu.HBM), pl.BlockSpec(memory_space=pltpu.VMEM)
    return pl.pallas_call(
        near_kernel,
        in_specs=[pl.BlockSpec(memory_space=pltpu.SMEM)] + [hbm] * 8,
        out_specs=[vmem] * 2,
        out_shape=[
            jax.ShapeDtypeStruct((width, both), jnp.bfloat16),
            jax.ShapeDtypeStruct((both // 2, width), jnp.float32),
        ],
        scratch_shapes=[
            pltpu.VMEM((2, 16, half, width), jnp.bfloat16),
            pltpu.VMEM((2, 16, half, width), jnp.bfloat16),
            pltpu.VMEM((rows, both // 2), jnp.bfloat16),
            pltpu.SemaphoreType.DMA((13,)),
        ],
        compiler_params=pltpu.CompilerParams(vmem_limit_bytes=60 << 20),
        cost_estimate=pl.CostEstimate(
            flops=3 * rows * both * width, bytes_accessed=4 * width * both * 2 + rows * width * 4, transcendentals=rows * both // 2
        ),
    )(starts, near, near_c, *blocks)


def far_kernel(line_ref, far, far_c, full_hbm, sums_hbm, *refs):
    outs = refs[:4]
    x_rows, y_rows, full, sums, hidden, sem = refs[4:]
    half = x_rows.shape[2]
    copies, begin = starter(sem)
    begin(full_hbm, full)
    for core, rows in enumerate((far, far_c)):
        begin(rows.at[:, :half, :], x_rows.at[core])
    for core, rows in enumerate((far, far_c)):
        begin(rows.at[:, half:, :], y_rows.at[core])
    begin(sums_hbm, sums)
    for copy in copies[:3]:
        copy.wait()
    gate_rows(x_rows, full, hidden)
    for copy in copies[3:]:
        copy.wait()
    y_all = y_rows.reshape(hidden.shape[0], full.shape[0])
    deep = outs[0].shape[0]
    for d in range(full.shape[0] // WIDE):
        cols = slice(d * WIDE, (d + 1) * WIDE)
        done = (sums[:, cols] + over_rows(hidden, y_all, cols)).astype(jnp.bfloat16)
        for line in range(4):

            @pl.when(line_ref[0] == line)
            def _(line=line, cols=cols, done=done):
                for s in range(4):
                    owner = (line + s) % 4
                    outs[s][:, cols] = done[owner * deep : (owner + 1) * deep, :]


def chunks(line, far, far_c, full, sums):
    half, width = far.shape[1] // 2, far.shape[2]
    units, rows = sums.shape[0], 32 * half
    hbm, vmem = pl.BlockSpec(memory_space=pltpu.HBM), pl.BlockSpec(memory_space=pltpu.VMEM)
    return pl.pallas_call(
        far_kernel,
        in_specs=[pl.BlockSpec(memory_space=pltpu.SMEM)] + [hbm] * 4,
        out_specs=[vmem] * 4,
        out_shape=[jax.ShapeDtypeStruct((units // 4, width), jnp.bfloat16)] * 4,
        scratch_shapes=[
            pltpu.VMEM((2, 16, half, width), jnp.bfloat16),
            pltpu.VMEM((2, 16, half, width), jnp.bfloat16),
            pltpu.VMEM(full.shape, jnp.bfloat16),
            pltpu.VMEM(sums.shape, jnp.float32),
            pltpu.VMEM((rows, units), jnp.bfloat16),
            pltpu.SemaphoreType.DMA((6,)),
        ],
        compiler_params=pltpu.CompilerParams(vmem_limit_bytes=60 << 20),
        cost_estimate=pl.CostEstimate(
            flops=6 * rows * units * width, bytes_accessed=10 * width * units + rows * width * 4, transcendentals=rows * units
        ),
    )(line, far, far_c, full, sums)


def pack_kernel(flag_ref, core_ref, gate_ref, up_ref, other_gate_ref, other_up_ref, mine_ref, theirs_ref):
    swapped = flag_ref[0] == 1
    units = gate_ref.shape[1]
    unit = lax.broadcasted_iota(jnp.int32, (units, units // 2), 0)
    column = lax.broadcasted_iota(jnp.int32, (units, units // 2), 1)
    for target, core in ((mine_ref, core_ref[0]), (theirs_ref, 1 - core_ref[0])):
        chosen = (unit == (column // 96 * 2 + core) * 96 + column % 96).astype(jnp.bfloat16)
        for at, here, there in ((0, gate_ref, other_gate_ref), (1, up_ref, other_up_ref)):
            held = jnp.where(swapped, there[...], here[...])
            target[:, at * units // 2 : (at + 1) * units // 2] = jnp.dot(
                held, chosen, preferred_element_type=jnp.float32
            ).astype(jnp.bfloat16)


def pack(flag, core, *matrices):
    smem, vmem = pl.BlockSpec(memory_space=pltpu.SMEM), pl.BlockSpec(memory_space=pltpu.VMEM)
    shape = jax.ShapeDtypeStruct(matrices[0].shape, jnp.bfloat16)
    return pl.pallas_call(
        pack_kernel, in_specs=[smem] * 2 + [vmem] * 4, out_specs=[vmem] * 2, out_shape=[shape] * 2
    )(flag, core, *matrices)


def together(*values):
    return lax.optimization_barrier(values)


def z_steps(step_of):
    pairs = []
    for line in range(4):
        to, by = step_of[line]
        pairs += [(line * 4 + hi, to * 4 + (hi + by) % 4) for hi in range(4)]
    return pairs


def shards(tokens, cotangent, w_gate, w_up, expert_ids, gate_num, swap_flags):
    tok_count, width = tokens.shape
    deep = w_gate.shape[1]
    ahead, back = [(i, (i + 1) % 4) for i in range(4)], [(i, (i - 1) % 4) for i in range(4)]
    opposite = [(i, (i + 2) % 4) for i in range(4)]
    cores = [(0, 1), (1, 0)]
    along_z = ("zl", "zh")
    first = z_steps([(0, 1), (2, -1), (1, 1), (3, -1)])
    second = z_steps([(2, -1), (0, 1), (3, -1), (1, 1)])
    onward = z_steps([(0, 1), (1, 1), (2, -1), (3, -1)])
    place, line, core = lax.axis_index("zh"), lax.axis_index("zl"), lax.axis_index("c")
    me = (lax.axis_index("x") * 4 + place) * 4 + lax.axis_index("y")
    select = functools.partial(route, swap_flags, place.reshape(1), width)
    meta = jnp.concatenate([expert_ids, gate_num], axis=1).astype(jnp.bfloat16)
    meta = jnp.pad(meta, ((0, tok_count), (0, 128 - meta.shape[1])))
    own = jnp.concatenate([jnp.concatenate([tokens, cotangent], axis=0), meta], axis=1)
    rows_a, rows_b = lax.ppermute(own, along_z, first), lax.ppermute(own, along_z, second)
    flag = lax.dynamic_slice(swap_flags, (me % 32,), (1,))
    mine, theirs = pack(
        flag,
        core.reshape(1),
        w_gate[0],
        w_up[0],
        lax.ppermute(w_gate[0], "x", opposite),
        lax.ppermute(w_up[0], "x", opposite),
    )
    block = jnp.concatenate([mine, lax.ppermute(theirs, "c", cores)], axis=0)
    near_send, rows_a = together(select([(own, own), (rows_a, rows_a), (rows_b, rows_b)]), rows_a)
    rows_f = lax.ppermute(rows_a, along_z, onward)
    block_l, block_r = lax.ppermute(block, "zl", ahead), lax.ppermute(block, "zl", back)
    early = deep // 4
    near, far_send, block_l, block_r, block_fr, block_fl = together(
        lax.all_to_all(near_send, PLANE, 0, 0, tiled=True),
        select([(rows_f, rows_f)]),
        block_l,
        block_r,
        lax.ppermute(block_r[deep:], "zl", back),
        lax.ppermute(block_l[:early], "zl", ahead),
    )
    rest_fl = lax.ppermute(block_l[early:deep], "zl", ahead)
    far = lax.all_to_all(far_send, PLANE, 0, 0, tiled=True)
    near_c = lax.ppermute(near, "c", cores)
    away = jnp.array([0, 0, 3, 3, 1, 1, 2, 2], jnp.int32)
    which = jnp.array([0, 1, 0, 1, 0, 1, 1, 0], jnp.int32)
    starts = (2 * ((line + away) % 4) + (core + which) % 2) * deep
    full, sums = near_sums(starts, near, near_c, [block, block_l, block_r, block_fr, block_fl, rest_fl])
    far, full, sums = together(far, full, sums)
    far_c = lax.ppermute(far, "c", cores)
    parts = chunks(line.reshape(1), far, far_c, full, sums)
    total = parts[0].astype(jnp.float32)
    for s in (2, 1, 3):
        total += lax.ppermute(parts[s], "zl", [(i, (i + s) % 4) for i in range(4)]).astype(jnp.float32)
    return total[None]


def solution(mesh):
    fine = Mesh(mesh.devices.reshape(4, 2, 4, 4, 4), ("zl", "c", "x", "zh", "y"))
    rows = P(("zl", "c", "x", "zh", "y"), None)
    split = P(("x", "zh", "y"), ("zl", "c"), None)
    in_specs = (rows, rows, split, split, rows, rows, P())
    return jax.shard_map(shards, mesh=fine, in_specs=in_specs, out_specs=split, check_vma=False)
```

```python
import functools

import jax
import jax.numpy as jnp
from jax import lax
from jax.experimental import pallas as pl
from jax.experimental.pallas import tpu as pltpu
from jax.sharding import Mesh, PartitionSpec as P

PLANE = ("x", "y")
RANKS = 8


def route_kernel(count, flags_ref, place_ref, *refs):
    metas, xs, ys = refs[:count], refs[count : 2 * count], refs[2 * count : 3 * count]
    out_ref, pick_ref, weigh_ref = refs[3 * count :]
    tok_count = metas[0].shape[0]
    slots = pick_ref.shape[2]

    @pl.when(pl.program_id(0) == 0)
    def _():
        lane = lax.broadcasted_iota(jnp.int32, (1, slots), 1)
        expert = jnp.zeros((1, slots), jnp.int32)
        for j in range(16):
            home = (j // 4) * 16 + place_ref[0] * 4 + j % 4
            other = lax.rem(home + 32, 64)
            held = jnp.where(flags_ref[lax.rem(home, 32)] == 1, other, home)
            expert = jnp.where(lane // RANKS == j, held, expert)
        expert = expert.astype(jnp.float32)
        rank_of = (lane % RANKS).astype(jnp.float32)
        earlier = (
            lax.broadcasted_iota(jnp.int32, (tok_count, tok_count), 0)
            > lax.broadcasted_iota(jnp.int32, (tok_count, tok_count), 1)
        ).astype(jnp.bfloat16)
        for s in range(count):
            meta = metas[s][...].astype(jnp.float32)
            weight = jnp.zeros((tok_count, slots), jnp.float32)
            for k in range(6):
                weight = jnp.where(meta[:, k : k + 1] == expert, meta[:, 6 + k : 7 + k], weight)
            chosen = jnp.where(weight > 0.0, 1.0, 0.0)
            before = jnp.dot(earlier, chosen.astype(jnp.bfloat16), preferred_element_type=jnp.float32)
            here = before == rank_of
            pick_ref[s] = jnp.where(here, chosen, 0.0).astype(jnp.bfloat16)
            weigh_ref[s] = jnp.where(here, weight * (1.0 / 64.0), 0.0).astype(jnp.bfloat16)

    for base, picks, rows in ((0, pick_ref, xs), (count, weigh_ref, ys)):
        for s in range(count):
            picked = lax.dot_general(
                picks[s], rows[s][...], (((0,), (0,)), ((), ())), preferred_element_type=jnp.float32
            )
            at = (base + s) * RANKS
            out_ref[:, at : at + RANKS, :] = picked.reshape(16, RANKS, picked.shape[1]).astype(jnp.bfloat16)


def route(flags, place, width, sources):
    count = len(sources)
    tok_count = 64
    tile = 512
    meta_block = width // 128
    smem = pl.BlockSpec(memory_space=pltpu.SMEM)
    x_of, y_of = [pair[0] for pair in sources], [pair[1] for pair in sources]
    y_block = 1 if x_of[0] is y_of[0] else 0
    return pl.pallas_call(
        functools.partial(route_kernel, count),
        grid=(width // tile,),
        in_specs=[smem] * 2
        + [pl.BlockSpec((tok_count, 128), lambda i: (0, meta_block))] * count
        + [pl.BlockSpec((tok_count, tile), lambda i: (0, i))] * count
        + [pl.BlockSpec((tok_count, tile), lambda i: (y_block, i))] * count,
        out_specs=pl.BlockSpec((16, 2 * count * RANKS, tile), lambda i: (0, 0, i)),
        out_shape=jax.ShapeDtypeStruct((16, 2 * count * RANKS, width), jnp.bfloat16),
        scratch_shapes=[pltpu.VMEM((count, tok_count, 16 * RANKS), jnp.bfloat16)] * 2,
        cost_estimate=pl.CostEstimate(
            flops=40_000_000_000,
            bytes_accessed=2 * count * (tok_count + 128) * width * 2,
            transcendentals=0,
        ),
    )(flags, place, *x_of, *x_of, *y_of)


def gate_rows(x_rows, full, hidden):
    total, units = hidden.shape
    x_all = x_rows.reshape(total, full.shape[0])
    tile = 256
    for m in range(total // tile):
        at = slice(m * tile, (m + 1) * tile)
        sums = jnp.dot(x_all[at, :], full[...], preferred_element_type=jnp.float32)
        hidden[at, :] = (jax.nn.silu(sums[:, :units]) * sums[:, units:]).astype(jnp.bfloat16)


def over_rows(hidden, y_rows, cols):
    return lax.dot_general(
        hidden[...], y_rows[:, cols], (((0,), (0,)), ((), ())), preferred_element_type=jnp.float32
    )


def starter(sem):
    copies = []

    def begin(source, target):
        copies.append(pltpu.make_async_copy(source, target, sem.at[len(copies)]))
        copies[-1].start()

    return copies, begin


WIDE = 512
TILE = 256


def pieces_of(blocks, starts_ref, base):
    deep = blocks[0].shape[0] // 2
    pieces = []
    for b, block in enumerate(blocks[:3]):
        for part in range(2):
            pieces.append((block.at[part * deep : (part + 1) * deep, :], starts_ref[2 * b + part] - base))
    for b, block in enumerate(blocks[3:]):
        past = blocks[4].shape[0] if b == 2 else 0
        pieces.append((block, starts_ref[min(6 + b, 7)] + past - base))
    return pieces


def place(begin, pieces, full):
    for piece, start in pieces:
        begin(piece, full.at[pl.ds(pl.multiple_of(start, 16), piece.shape[0]), :])


def early_kernel(starts_ref, bases_ref, near, near_c, b0, b1, b2, sums_ref, x_rows, full, sem):
    half = x_rows.shape[2]
    copies, begin = starter(sem)
    begin(near.at[:, :half, :], x_rows.at[0])
    begin(near_c.at[:, :half, :], x_rows.at[1])
    place(begin, pieces_of((b0, b1, b2), starts_ref, 0), full)
    for copy in copies:
        copy.wait()
    total, chunk = sums_ref.shape[0], b0.shape[0]
    x_all = x_rows.reshape(total, full.shape[0])
    for m in range(total // TILE):
        at = slice(m * TILE, (m + 1) * TILE)
        sums = None
        for b in range(3):
            here = pl.ds(pl.multiple_of(bases_ref[b], 128), chunk)
            part = jnp.dot(x_all[at, here], full[here, :], preferred_element_type=jnp.float32)
            sums = part if sums is None else sums + part
        sums_ref[at, :] = sums


def hidden_kernel(starts_ref, bases_ref, near, near_c, b3, b4, b5, sums_hbm, hidden_ref, x_rows, full, sums, sem):
    half, chunk = x_rows.shape[2], x_rows.shape[3]
    copies, begin = starter(sem)
    base = pl.multiple_of(bases_ref[3], 128)
    begin(near.at[:, :half, pl.ds(base, chunk)], x_rows.at[0])
    begin(near_c.at[:, :half, pl.ds(base, chunk)], x_rows.at[1])
    place(begin, [(b3, starts_ref[6] - base), (b4, starts_ref[7] - base), (b5, starts_ref[7] - base + b4.shape[0])], full)
    begin(sums_hbm, sums)
    for copy in copies:
        copy.wait()
    total, units = hidden_ref.shape
    x_all = x_rows.reshape(total, chunk)
    for m in range(total // TILE):
        at = slice(m * TILE, (m + 1) * TILE)
        both = sums[at, :] + jnp.dot(x_all[at, :], full[...], preferred_element_type=jnp.float32)
        hidden_ref[at, :] = (jax.nn.silu(both[:, :units]) * both[:, units:]).astype(jnp.bfloat16)


def near_kernel(near, near_c, hidden, sums_ref, y_rows, sem):
    half = y_rows.shape[2]
    copies, begin = starter(sem)
    begin(near.at[:, half:, :], y_rows.at[0])
    begin(near_c.at[:, half:, :], y_rows.at[1])
    for copy in copies:
        copy.wait()
    y_all = y_rows.reshape(hidden.shape[0], sums_ref.shape[1])
    for d in range(sums_ref.shape[1] // WIDE):
        cols = slice(d * WIDE, (d + 1) * WIDE)
        sums_ref[:, cols] = over_rows(hidden, y_all, cols)


def far_kernel(starts_ref, line_ref, far, far_c, b0, b1, b2, b3, b4, b5, sums_hbm, *refs):
    outs = refs[:4]
    x_rows, y_rows, full, sums, hidden, sem = refs[4:]
    half = x_rows.shape[2]
    copies, begin = starter(sem)
    place(begin, pieces_of((b0, b1, b2, b3, b4, b5), starts_ref, 0), full)
    for core, rows in enumerate((far, far_c)):
        begin(rows.at[:, :half, :], x_rows.at[core])
    for core, rows in enumerate((far, far_c)):
        begin(rows.at[:, half:, :], y_rows.at[core])
    begin(sums_hbm, sums)
    for copy in copies[:-3]:
        copy.wait()
    gate_rows(x_rows, full, hidden)
    for copy in copies[-3:]:
        copy.wait()
    y_all = y_rows.reshape(hidden.shape[0], full.shape[0])
    deep = outs[0].shape[0]
    for d in range(full.shape[0] // WIDE):
        cols = slice(d * WIDE, (d + 1) * WIDE)
        done = (sums[:, cols] + over_rows(hidden, y_all, cols)).astype(jnp.bfloat16)
        for line in range(4):

            @pl.when(line_ref[0] == line)
            def _(line=line, cols=cols, done=done):
                for s in range(4):
                    owner = (line + s) % 4
                    outs[s][:, cols] = done[owner * deep : (owner + 1) * deep, :]


def call(body, smems, hbms, vmems, outs, scratch, flops, moved):
    smem, vmem = pl.BlockSpec(memory_space=pltpu.SMEM), pl.BlockSpec(memory_space=pltpu.VMEM)
    hbm = pl.BlockSpec(memory_space=pltpu.HBM)
    return pl.pallas_call(
        body,
        in_specs=[smem] * len(smems) + [hbm] * len(hbms) + [vmem] * len(vmems),
        out_specs=[vmem] * len(outs),
        out_shape=outs,
        scratch_shapes=scratch,
        compiler_params=pltpu.CompilerParams(vmem_limit_bytes=60 << 20),
        cost_estimate=pl.CostEstimate(flops=flops, bytes_accessed=moved, transcendentals=0),
    )(*smems, *hbms, *vmems)


def rows_of(half, width):
    return pltpu.VMEM((2, 16, half, width), jnp.bfloat16)


def early_sums(starts, bases, near, near_c, blocks):
    half, width, both = near.shape[1] // 2, near.shape[2], blocks[0].shape[1]
    rows = 32 * half
    return call(
        early_kernel, (starts, bases), (near, near_c, *blocks[:3]), (),
        [jax.ShapeDtypeStruct((rows, both), jnp.float32)],
        [rows_of(half, width), pltpu.VMEM((width, both), jnp.bfloat16), pltpu.SemaphoreType.DMA((8,))],
        rows * both * width * 3 // 2, 2 * rows * width + 2 * width * both + 4 * rows * both,
    )[0]


def hidden_near(starts, bases, near, near_c, blocks, sums):
    half, chunk, both = near.shape[1] // 2, blocks[0].shape[0], blocks[0].shape[1]
    rows = 32 * half
    return call(
        hidden_kernel, (starts, bases), (near, near_c, *blocks[3:], sums), (),
        [jax.ShapeDtypeStruct((rows, both // 2), jnp.bfloat16)],
        [
            rows_of(half, chunk), pltpu.VMEM((chunk, both), jnp.bfloat16), pltpu.VMEM((rows, both), jnp.float32),
            pltpu.SemaphoreType.DMA((6,)),
        ],
        2 * rows * both * chunk, 2 * (rows + both) * chunk + 5 * rows * both,
    )[0]


def near_sums(near, near_c, hidden):
    half, width = near.shape[1] // 2, near.shape[2]
    rows, units = hidden.shape
    return call(
        near_kernel, (), (near, near_c), (hidden,), [jax.ShapeDtypeStruct((units, width), jnp.float32)],
        [rows_of(half, width), pltpu.SemaphoreType.DMA((2,))],
        2 * rows * units * width, 2 * rows * (width + units) + 4 * units * width,
    )[0]


def chunks(starts, line, far, far_c, blocks, sums):
    half, width = far.shape[1] // 2, far.shape[2]
    units, rows = sums.shape[0], 32 * half
    return call(
        far_kernel, (starts, line), (far, far_c, *blocks, sums), (),
        [jax.ShapeDtypeStruct((units // 4, width), jnp.bfloat16)] * 4,
        [
            rows_of(half, width), rows_of(half, width), pltpu.VMEM((width, 2 * units), jnp.bfloat16),
            pltpu.VMEM(sums.shape, jnp.float32), pltpu.VMEM((rows, units), jnp.bfloat16), pltpu.SemaphoreType.DMA((14,)),
        ],
        6 * rows * units * width, 10 * width * units + rows * width * 4,
    )


def pack_kernel(flag_ref, core_ref, gate_ref, up_ref, other_gate_ref, other_up_ref, mine_ref, theirs_ref):
    swapped = flag_ref[0] == 1
    units = gate_ref.shape[1]
    unit = lax.broadcasted_iota(jnp.int32, (units, units // 2), 0)
    column = lax.broadcasted_iota(jnp.int32, (units, units // 2), 1)
    for target, core in ((mine_ref, core_ref[0]), (theirs_ref, 1 - core_ref[0])):
        chosen = (unit == (column // 96 * 2 + core) * 96 + column % 96).astype(jnp.bfloat16)
        for at, here, there in ((0, gate_ref, other_gate_ref), (1, up_ref, other_up_ref)):
            held = jnp.where(swapped, there[...], here[...])
            target[:, at * units // 2 : (at + 1) * units // 2] = jnp.dot(
                held, chosen, preferred_element_type=jnp.float32
            ).astype(jnp.bfloat16)


def pack(flag, core, *matrices):
    smem, vmem = pl.BlockSpec(memory_space=pltpu.SMEM), pl.BlockSpec(memory_space=pltpu.VMEM)
    shape = jax.ShapeDtypeStruct(matrices[0].shape, jnp.bfloat16)
    return pl.pallas_call(
        pack_kernel, in_specs=[smem] * 2 + [vmem] * 4, out_specs=[vmem] * 2, out_shape=[shape] * 2
    )(flag, core, *matrices)


def together(*values):
    return lax.optimization_barrier(values)


def z_steps(step_of):
    pairs = []
    for line in range(4):
        to, by = step_of[line]
        pairs += [(line * 4 + hi, to * 4 + (hi + by) % 4) for hi in range(4)]
    return pairs


def shards(tokens, cotangent, w_gate, w_up, expert_ids, gate_num, swap_flags):
    tok_count, width = tokens.shape
    deep = w_gate.shape[1]
    ahead, back = [(i, (i + 1) % 4) for i in range(4)], [(i, (i - 1) % 4) for i in range(4)]
    opposite = [(i, (i + 2) % 4) for i in range(4)]
    cores = [(0, 1), (1, 0)]
    along_z = ("zl", "zh")
    first = z_steps([(0, 1), (2, -1), (1, 1), (3, -1)])
    second = z_steps([(2, -1), (0, 1), (3, -1), (1, 1)])
    onward = z_steps([(0, 1), (1, 1), (2, -1), (3, -1)])
    place, line, core = lax.axis_index("zh"), lax.axis_index("zl"), lax.axis_index("c")
    me = (lax.axis_index("x") * 4 + place) * 4 + lax.axis_index("y")
    select = functools.partial(route, swap_flags, place.reshape(1), width)
    meta = jnp.concatenate([expert_ids, gate_num], axis=1).astype(jnp.bfloat16)
    meta = jnp.pad(meta, ((0, tok_count), (0, 128 - meta.shape[1])))
    own = jnp.concatenate([jnp.concatenate([tokens, cotangent], axis=0), meta], axis=1)
    rows_a, rows_b = lax.ppermute(own, along_z, first), lax.ppermute(own, along_z, second)
    flag = lax.dynamic_slice(swap_flags, (me % 32,), (1,))
    mine, theirs = pack(
        flag,
        core.reshape(1),
        w_gate[0],
        w_up[0],
        lax.ppermute(w_gate[0], "x", opposite),
        lax.ppermute(w_up[0], "x", opposite),
    )
    block = jnp.concatenate([mine, lax.ppermute(theirs, "c", cores)], axis=0)
    near_send, rows_a = together(select([(own, own), (rows_a, rows_a), (rows_b, rows_b)]), rows_a)
    rows_f = lax.ppermute(rows_a, along_z, onward)
    block_l, block_r = lax.ppermute(block, "zl", ahead), lax.ppermute(block, "zl", back)
    early = deep + deep // 4
    near, far_send, block_l, block_r, block_fl, block_fr = together(
        lax.all_to_all(near_send, PLANE, 0, 0, tiled=True),
        select([(rows_f, rows_f)]),
        block_l,
        block_r,
        lax.ppermute(block_l[:deep], "zl", ahead),
        lax.ppermute(block_r[deep:early], "zl", back),
    )
    rest_fr = lax.ppermute(block_r[early:], "zl", back)
    far = lax.all_to_all(far_send, PLANE, 0, 0, tiled=True)
    near_c = lax.ppermute(near, "c", cores)
    away = jnp.array([0, 0, 3, 3, 1, 1, 2, 2], jnp.int32)
    which = jnp.array([0, 1, 0, 1, 0, 1, 0, 1], jnp.int32)
    starts = (2 * ((line + away) % 4) + (core + which) % 2) * deep
    bases = (line + jnp.array([0, 3, 1, 2], jnp.int32)) % 4 * (2 * deep)
    blocks = [block, block_l, block_r, block_fl, block_fr, rest_fr]
    sums = early_sums(starts, bases, near, near_c, blocks)
    hidden = hidden_near(starts, bases, near, near_c, blocks, sums)
    far, hidden = together(far, hidden)
    far_c = lax.ppermute(far, "c", cores)
    parts = chunks(starts, line.reshape(1), far, far_c, blocks, near_sums(near, near_c, hidden))
    total = parts[0].astype(jnp.float32)
    for s in (2, 1, 3):
        total += lax.ppermute(parts[s], "zl", [(i, (i + s) % 4) for i in range(4)]).astype(jnp.float32)
    return total[None]


def solution(mesh):
    fine = Mesh(mesh.devices.reshape(4, 2, 4, 4, 4), ("zl", "c", "x", "zh", "y"))
    rows = P(("zl", "c", "x", "zh", "y"), None)
    split = P(("x", "zh", "y"), ("zl", "c"), None)
    in_specs = (rows, rows, split, split, rows, rows, P())
    return jax.shard_map(shards, mesh=fine, in_specs=in_specs, out_specs=split, check_vma=False)
```

```python
import functools

import jax
import jax.numpy as jnp
from jax import lax
from jax.experimental import pallas as pl
from jax.experimental.pallas import tpu as pltpu
from jax.sharding import Mesh, PartitionSpec as P

PLANE = ("x", "y")
RANKS = 8


def route_kernel(count, flags_ref, place_ref, *refs):
    metas, xs, ys = refs[:count], refs[count : 2 * count], refs[2 * count : 3 * count]
    out_ref, pick_ref, weigh_ref = refs[3 * count :]
    tok_count = metas[0].shape[0]
    slots = pick_ref.shape[2]

    @pl.when(pl.program_id(0) == 0)
    def _():
        lane = lax.broadcasted_iota(jnp.int32, (1, slots), 1)
        expert = jnp.zeros((1, slots), jnp.int32)
        for j in range(16):
            home = (j // 4) * 16 + place_ref[0] * 4 + j % 4
            other = lax.rem(home + 32, 64)
            held = jnp.where(flags_ref[lax.rem(home, 32)] == 1, other, home)
            expert = jnp.where(lane // RANKS == j, held, expert)
        expert = expert.astype(jnp.float32)
        rank_of = (lane % RANKS).astype(jnp.float32)
        earlier = (
            lax.broadcasted_iota(jnp.int32, (tok_count, tok_count), 0)
            > lax.broadcasted_iota(jnp.int32, (tok_count, tok_count), 1)
        ).astype(jnp.bfloat16)
        for s in range(count):
            meta = metas[s][...].astype(jnp.float32)
            weight = jnp.zeros((tok_count, slots), jnp.float32)
            for k in range(6):
                weight = jnp.where(meta[:, k : k + 1] == expert, meta[:, 6 + k : 7 + k], weight)
            chosen = jnp.where(weight > 0.0, 1.0, 0.0)
            before = jnp.dot(earlier, chosen.astype(jnp.bfloat16), preferred_element_type=jnp.float32)
            here = before == rank_of
            pick_ref[s] = jnp.where(here, chosen, 0.0).astype(jnp.bfloat16)
            weigh_ref[s] = jnp.where(here, weight * (1.0 / 64.0), 0.0).astype(jnp.bfloat16)

    for base, picks, rows in ((0, pick_ref, xs), (count, weigh_ref, ys)):
        for s in range(count):
            picked = lax.dot_general(
                picks[s], rows[s][...], (((0,), (0,)), ((), ())), preferred_element_type=jnp.float32
            )
            at = (base + s) * RANKS
            out_ref[:, at : at + RANKS, :] = picked.reshape(16, RANKS, picked.shape[1]).astype(jnp.bfloat16)


def route(flags, place, width, sources):
    count = len(sources)
    tok_count = 64
    tile = 512
    meta_block = width // 128
    smem = pl.BlockSpec(memory_space=pltpu.SMEM)
    x_of, y_of = [pair[0] for pair in sources], [pair[1] for pair in sources]
    y_block = 1 if x_of[0] is y_of[0] else 0
    return pl.pallas_call(
        functools.partial(route_kernel, count),
        grid=(width // tile,),
        in_specs=[smem] * 2
        + [pl.BlockSpec((tok_count, 128), lambda i: (0, meta_block))] * count
        + [pl.BlockSpec((tok_count, tile), lambda i: (0, i))] * count
        + [pl.BlockSpec((tok_count, tile), lambda i: (y_block, i))] * count,
        out_specs=pl.BlockSpec((16, 2 * count * RANKS, tile), lambda i: (0, 0, i)),
        out_shape=jax.ShapeDtypeStruct((16, 2 * count * RANKS, width), jnp.bfloat16),
        scratch_shapes=[pltpu.VMEM((count, tok_count, 16 * RANKS), jnp.bfloat16)] * 2,
        cost_estimate=pl.CostEstimate(
            flops=40_000_000_000,
            bytes_accessed=2 * count * (tok_count + 128) * width * 2,
            transcendentals=0,
        ),
    )(flags, place, *x_of, *x_of, *y_of)


def gate_rows(x_rows, full, hidden):
    total, units = hidden.shape
    x_all = x_rows.reshape(total, full.shape[0])
    tile = 256
    for m in range(total // tile):
        at = slice(m * tile, (m + 1) * tile)
        sums = jnp.dot(x_all[at, :], full[...], preferred_element_type=jnp.float32)
        hidden[at, :] = (jax.nn.silu(sums[:, :units]) * sums[:, units:]).astype(jnp.bfloat16)


def over_rows(hidden, y_rows, cols):
    return lax.dot_general(
        hidden[...], y_rows[:, cols], (((0,), (0,)), ((), ())), preferred_element_type=jnp.float32
    )


def starter(sem):
    copies = []

    def begin(source, target):
        copies.append(pltpu.make_async_copy(source, target, sem.at[len(copies)]))
        copies[-1].start()

    return copies, begin


WIDE = 512
TILE = 256


def pieces_of(blocks, starts_ref, base):
    deep = blocks[0].shape[0] // 2
    pieces = []
    for b, block in enumerate(blocks[:3]):
        for part in range(2):
            pieces.append((block.at[part * deep : (part + 1) * deep, :], starts_ref[2 * b + part] - base))
    for b, block in enumerate(blocks[3:]):
        past = blocks[4].shape[0] if b == 2 else 0
        pieces.append((block, starts_ref[min(6 + b, 7)] + past - base))
    return pieces


def place(begin, pieces, full):
    for piece, start in pieces:
        begin(piece, full.at[pl.ds(pl.multiple_of(start, 16), piece.shape[0]), :])


def early_kernel(starts_ref, bases_ref, near, near_c, b0, b1, b2, sums_ref, x_rows, full, sem):
    half = x_rows.shape[2]
    copies, begin = starter(sem)
    begin(near.at[:, :half, :], x_rows.at[0])
    begin(near_c.at[:, :half, :], x_rows.at[1])
    place(begin, pieces_of((b0, b1, b2), starts_ref, 0), full)
    for copy in copies:
        copy.wait()
    total, chunk = sums_ref.shape[0], b0.shape[0]
    x_all = x_rows.reshape(total, full.shape[0])
    for m in range(total // TILE):
        at = slice(m * TILE, (m + 1) * TILE)
        sums = None
        for b in range(3):
            here = pl.ds(pl.multiple_of(bases_ref[b], 128), chunk)
            part = jnp.dot(x_all[at, here], full[here, :], preferred_element_type=jnp.float32)
            sums = part if sums is None else sums + part
        sums_ref[at, :] = sums


def hidden_kernel(starts_ref, bases_ref, near, near_c, b3, b4, b5, sums_hbm, hidden_ref, x_rows, full, sums, sem):
    half, chunk = x_rows.shape[2], x_rows.shape[3]
    copies, begin = starter(sem)
    base = pl.multiple_of(bases_ref[3], 128)
    begin(near.at[:, :half, pl.ds(base, chunk)], x_rows.at[0])
    begin(near_c.at[:, :half, pl.ds(base, chunk)], x_rows.at[1])
    place(begin, [(b3, starts_ref[6] - base), (b4, starts_ref[7] - base), (b5, starts_ref[7] - base + b4.shape[0])], full)
    begin(sums_hbm, sums)
    for copy in copies:
        copy.wait()
    total, units = hidden_ref.shape
    x_all = x_rows.reshape(total, chunk)
    for m in range(total // TILE):
        at = slice(m * TILE, (m + 1) * TILE)
        both = sums[at, :] + jnp.dot(x_all[at, :], full[...], preferred_element_type=jnp.float32)
        hidden_ref[at, :] = (jax.nn.silu(both[:, :units]) * both[:, units:]).astype(jnp.bfloat16)


def last_kernel(starts_ref, line_ref, far, far_c, near, near_c, b0, b1, b2, b3, b4, b5, hidden_near, *refs):
    outs = refs[:4]
    x_rows, y_far, y_near, full, hidden_far, sem = refs[4:]
    half, n_half = x_rows.shape[2], y_near.shape[2]
    copies, begin = starter(sem)
    place(begin, pieces_of((b0, b1, b2, b3, b4, b5), starts_ref, 0), full)
    for core, rows in enumerate((far, far_c)):
        begin(rows.at[:, :half, :], x_rows.at[core])
    for core, rows in enumerate((near, near_c)):
        begin(rows.at[:, n_half:, :], y_near.at[core])
    for core, rows in enumerate((far, far_c)):
        begin(rows.at[:, half:, :], y_far.at[core])
    for copy in copies[:-4]:
        copy.wait()
    gate_rows(x_rows, full, hidden_far)
    for copy in copies[-4:]:
        copy.wait()
    width = full.shape[0]
    y_n, y_f = y_near.reshape(hidden_near.shape[0], width), y_far.reshape(hidden_far.shape[0], width)
    deep = outs[0].shape[0]
    for d in range(width // WIDE):
        cols = slice(d * WIDE, (d + 1) * WIDE)
        done = (over_rows(hidden_near, y_n, cols) + over_rows(hidden_far, y_f, cols)).astype(jnp.bfloat16)
        for line in range(4):

            @pl.when(line_ref[0] == line)
            def _(line=line, cols=cols, done=done):
                for s in range(4):
                    owner = (line + s) % 4
                    outs[s][:, cols] = done[owner * deep : (owner + 1) * deep, :]


def call(body, smems, hbms, vmems, outs, scratch, flops, moved, grant=60):
    smem, vmem = pl.BlockSpec(memory_space=pltpu.SMEM), pl.BlockSpec(memory_space=pltpu.VMEM)
    hbm = pl.BlockSpec(memory_space=pltpu.HBM)
    return pl.pallas_call(
        body,
        in_specs=[smem] * len(smems) + [hbm] * len(hbms) + [vmem] * len(vmems),
        out_specs=[vmem] * len(outs),
        out_shape=outs,
        scratch_shapes=scratch,
        compiler_params=pltpu.CompilerParams(vmem_limit_bytes=grant << 20),
        cost_estimate=pl.CostEstimate(flops=flops, bytes_accessed=moved, transcendentals=0),
    )(*smems, *hbms, *vmems)


def rows_of(half, width):
    return pltpu.VMEM((2, 16, half, width), jnp.bfloat16)


def early_sums(starts, bases, near, near_c, blocks):
    half, width, both = near.shape[1] // 2, near.shape[2], blocks[0].shape[1]
    rows = 32 * half
    return call(
        early_kernel, (starts, bases), (near, near_c, *blocks[:3]), (),
        [jax.ShapeDtypeStruct((rows, both), jnp.float32)],
        [rows_of(half, width), pltpu.VMEM((width, both), jnp.bfloat16), pltpu.SemaphoreType.DMA((8,))],
        rows * both * width * 3 // 2, 2 * rows * width + 2 * width * both + 4 * rows * both,
    )[0]


def hidden_near(starts, bases, near, near_c, blocks, sums):
    half, chunk, both = near.shape[1] // 2, blocks[0].shape[0], blocks[0].shape[1]
    rows = 32 * half
    return call(
        hidden_kernel, (starts, bases), (near, near_c, *blocks[3:], sums), (),
        [jax.ShapeDtypeStruct((rows, both // 2), jnp.bfloat16)],
        [
            rows_of(half, chunk), pltpu.VMEM((chunk, both), jnp.bfloat16), pltpu.VMEM((rows, both), jnp.float32),
            pltpu.SemaphoreType.DMA((6,)),
        ],
        2 * rows * both * chunk, 2 * (rows + both) * chunk + 5 * rows * both,
    )[0]


def chunks(starts, line, far, far_c, near, near_c, blocks, hidden):
    f_half, n_half, width = far.shape[1] // 2, near.shape[1] // 2, far.shape[2]
    units, rows = hidden.shape[1], 32 * (f_half + n_half)
    return call(
        last_kernel, (starts, line), (far, far_c, near, near_c, *blocks), (hidden,),
        [jax.ShapeDtypeStruct((units // 4, width), jnp.bfloat16)] * 4,
        [
            rows_of(f_half, width), rows_of(f_half, width), rows_of(n_half, width),
            pltpu.VMEM((width, 2 * units), jnp.bfloat16), pltpu.VMEM((32 * f_half, units), jnp.bfloat16),
            pltpu.SemaphoreType.DMA((15,)),
        ],
        2 * rows * units * width + 128 * f_half * units * width, 6 * width * units + rows * width * 2, 60,
    )


def pack_kernel(flag_ref, core_ref, gate_ref, up_ref, other_gate_ref, other_up_ref, mine_ref, theirs_ref):
    swapped = flag_ref[0] == 1
    units = gate_ref.shape[1]
    unit = lax.broadcasted_iota(jnp.int32, (units, units // 2), 0)
    column = lax.broadcasted_iota(jnp.int32, (units, units // 2), 1)
    for target, core in ((mine_ref, core_ref[0]), (theirs_ref, 1 - core_ref[0])):
        chosen = (unit == (column // 96 * 2 + core) * 96 + column % 96).astype(jnp.bfloat16)
        for at, here, there in ((0, gate_ref, other_gate_ref), (1, up_ref, other_up_ref)):
            held = jnp.where(swapped, there[...], here[...])
            target[:, at * units // 2 : (at + 1) * units // 2] = jnp.dot(
                held, chosen, preferred_element_type=jnp.float32
            ).astype(jnp.bfloat16)


def pack(flag, core, *matrices):
    smem, vmem = pl.BlockSpec(memory_space=pltpu.SMEM), pl.BlockSpec(memory_space=pltpu.VMEM)
    shape = jax.ShapeDtypeStruct(matrices[0].shape, jnp.bfloat16)
    return pl.pallas_call(
        pack_kernel, in_specs=[smem] * 2 + [vmem] * 4, out_specs=[vmem] * 2, out_shape=[shape] * 2
    )(flag, core, *matrices)


def together(*values):
    return lax.optimization_barrier(values)


def z_steps(step_of):
    pairs = []
    for line in range(4):
        to, by = step_of[line]
        pairs += [(line * 4 + hi, to * 4 + (hi + by) % 4) for hi in range(4)]
    return pairs


def shards(tokens, cotangent, w_gate, w_up, expert_ids, gate_num, swap_flags):
    tok_count, width = tokens.shape
    deep = w_gate.shape[1]
    ahead, back = [(i, (i + 1) % 4) for i in range(4)], [(i, (i - 1) % 4) for i in range(4)]
    opposite = [(i, (i + 2) % 4) for i in range(4)]
    cores = [(0, 1), (1, 0)]
    along_z = ("zl", "zh")
    first = z_steps([(0, 1), (2, -1), (1, 1), (3, -1)])
    second = z_steps([(2, -1), (0, 1), (3, -1), (1, 1)])
    onward = z_steps([(0, 1), (1, 1), (2, -1), (3, -1)])
    place, line, core = lax.axis_index("zh"), lax.axis_index("zl"), lax.axis_index("c")
    me = (lax.axis_index("x") * 4 + place) * 4 + lax.axis_index("y")
    select = functools.partial(route, swap_flags, place.reshape(1), width)
    meta = jnp.concatenate([expert_ids, gate_num], axis=1).astype(jnp.bfloat16)
    meta = jnp.pad(meta, ((0, tok_count), (0, 128 - meta.shape[1])))
    own = jnp.concatenate([jnp.concatenate([tokens, cotangent], axis=0), meta], axis=1)
    rows_a, rows_b = lax.ppermute(own, along_z, first), lax.ppermute(own, along_z, second)
    flag = lax.dynamic_slice(swap_flags, (me % 32,), (1,))
    mine, theirs = pack(
        flag,
        core.reshape(1),
        w_gate[0],
        w_up[0],
        lax.ppermute(w_gate[0], "x", opposite),
        lax.ppermute(w_up[0], "x", opposite),
    )
    block = jnp.concatenate([mine, lax.ppermute(theirs, "c", cores)], axis=0)
    near_send, rows_a = together(select([(own, own), (rows_a, rows_a), (rows_b, rows_b)]), rows_a)
    rows_f = lax.ppermute(rows_a, along_z, onward)
    block_l, block_r = lax.ppermute(block, "zl", ahead), lax.ppermute(block, "zl", back)
    early = deep + deep // 4
    near, far_send, block_l, block_r, block_fl, block_fr = together(
        lax.all_to_all(near_send, PLANE, 0, 0, tiled=True),
        select([(rows_f, rows_f)]),
        block_l,
        block_r,
        lax.ppermute(block_l[:deep], "zl", ahead),
        lax.ppermute(block_r[deep:early], "zl", back),
    )
    rest_fr = lax.ppermute(block_r[early:], "zl", back)
    far = lax.all_to_all(far_send, PLANE, 0, 0, tiled=True)
    near_c = lax.ppermute(near, "c", cores)
    away = jnp.array([0, 0, 3, 3, 1, 1, 2, 2], jnp.int32)
    which = jnp.array([0, 1, 0, 1, 0, 1, 0, 1], jnp.int32)
    starts = (2 * ((line + away) % 4) + (core + which) % 2) * deep
    bases = (line + jnp.array([0, 3, 1, 2], jnp.int32)) % 4 * (2 * deep)
    blocks = [block, block_l, block_r, block_fl, block_fr, rest_fr]
    sums = early_sums(starts, bases, near, near_c, blocks)
    hidden = hidden_near(starts, bases, near, near_c, blocks, sums)
    far, hidden = together(far, hidden)
    far_c = lax.ppermute(far, "c", cores)
    parts = chunks(starts, line.reshape(1), far, far_c, near, near_c, blocks, hidden)
    total = parts[0].astype(jnp.float32)
    for s in (2, 1, 3):
        total += lax.ppermute(parts[s], "zl", [(i, (i + s) % 4) for i in range(4)]).astype(jnp.float32)
    return total[None]


def solution(mesh):
    fine = Mesh(mesh.devices.reshape(4, 2, 4, 4, 4), ("zl", "c", "x", "zh", "y"))
    rows = P(("zl", "c", "x", "zh", "y"), None)
    split = P(("x", "zh", "y"), ("zl", "c"), None)
    in_specs = (rows, rows, split, split, rows, rows, P())
    return jax.shard_map(shards, mesh=fine, in_specs=in_specs, out_specs=split, check_vma=False)
```

```python
import functools

import jax
import jax.numpy as jnp
from jax import lax
from jax.experimental import pallas as pl
from jax.experimental.pallas import tpu as pltpu
from jax.sharding import Mesh, PartitionSpec as P

PLANE = ("x", "y")
RANKS = 8


def route_kernel(count, flags_ref, place_ref, *refs):
    metas, xs, ys = refs[:count], refs[count : 2 * count], refs[2 * count : 3 * count]
    out_ref, pick_ref, weigh_ref = refs[3 * count :]
    tok_count = metas[0].shape[0]
    slots = pick_ref.shape[2]

    @pl.when(pl.program_id(0) == 0)
    def _():
        lane = lax.broadcasted_iota(jnp.int32, (1, slots), 1)
        expert = jnp.zeros((1, slots), jnp.int32)
        for j in range(16):
            home = (j // 4) * 16 + place_ref[0] * 4 + j % 4
            other = lax.rem(home + 32, 64)
            held = jnp.where(flags_ref[lax.rem(home, 32)] == 1, other, home)
            expert = jnp.where(lane // RANKS == j, held, expert)
        expert = expert.astype(jnp.float32)
        rank_of = (lane % RANKS).astype(jnp.float32)
        earlier = (
            lax.broadcasted_iota(jnp.int32, (tok_count, tok_count), 0)
            > lax.broadcasted_iota(jnp.int32, (tok_count, tok_count), 1)
        ).astype(jnp.bfloat16)
        for s in range(count):
            meta = metas[s][...].astype(jnp.float32)
            weight = jnp.zeros((tok_count, slots), jnp.float32)
            for k in range(6):
                weight = jnp.where(meta[:, k : k + 1] == expert, meta[:, 6 + k : 7 + k], weight)
            chosen = jnp.where(weight > 0.0, 1.0, 0.0)
            before = jnp.dot(earlier, chosen.astype(jnp.bfloat16), preferred_element_type=jnp.float32)
            here = before == rank_of
            pick_ref[s] = jnp.where(here, chosen, 0.0).astype(jnp.bfloat16)
            weigh_ref[s] = jnp.where(here, weight * (1.0 / 64.0), 0.0).astype(jnp.bfloat16)

    for base, picks, rows in ((0, pick_ref, xs), (count, weigh_ref, ys)):
        for s in range(count):
            picked = lax.dot_general(
                picks[s], rows[s][...], (((0,), (0,)), ((), ())), preferred_element_type=jnp.float32
            )
            at = (base + s) * RANKS
            out_ref[:, at : at + RANKS, :] = picked.reshape(16, RANKS, picked.shape[1]).astype(jnp.bfloat16)


def route(flags, place, width, sources):
    count = len(sources)
    tok_count = 64
    tile = 512
    meta_block = width // 128
    smem = pl.BlockSpec(memory_space=pltpu.SMEM)
    x_of, y_of = [pair[0] for pair in sources], [pair[1] for pair in sources]
    y_block = 1 if x_of[0] is y_of[0] else 0
    return pl.pallas_call(
        functools.partial(route_kernel, count),
        grid=(width // tile,),
        in_specs=[smem] * 2
        + [pl.BlockSpec((tok_count, 128), lambda i: (0, meta_block))] * count
        + [pl.BlockSpec((tok_count, tile), lambda i: (0, i))] * count
        + [pl.BlockSpec((tok_count, tile), lambda i: (y_block, i))] * count,
        out_specs=pl.BlockSpec((16, 2 * count * RANKS, tile), lambda i: (0, 0, i)),
        out_shape=jax.ShapeDtypeStruct((16, 2 * count * RANKS, width), jnp.bfloat16),
        scratch_shapes=[pltpu.VMEM((count, tok_count, 16 * RANKS), jnp.bfloat16)] * 2,
        cost_estimate=pl.CostEstimate(
            flops=40_000_000_000,
            bytes_accessed=2 * count * (tok_count + 128) * width * 2,
            transcendentals=0,
        ),
    )(flags, place, *x_of, *x_of, *y_of)


def gate_rows(x_rows, full, hidden):
    total, units = hidden.shape
    x_all = x_rows.reshape(total, full.shape[0])
    tile = 256
    for m in range(total // tile):
        at = slice(m * tile, (m + 1) * tile)
        sums = jnp.dot(x_all[at, :], full[...], preferred_element_type=jnp.float32)
        hidden[at, :] = (jax.nn.silu(sums[:, :units]) * sums[:, units:]).astype(jnp.bfloat16)


def over_rows(hidden, y_rows, cols):
    return lax.dot_general(
        hidden[...], y_rows[:, cols], (((0,), (0,)), ((), ())), preferred_element_type=jnp.float32
    )


def starter(sem):
    copies = []

    def begin(source, target):
        copies.append(pltpu.make_async_copy(source, target, sem.at[len(copies)]))
        copies[-1].start()

    return copies, begin


WIDE = 512
TILE = 256


def pieces_of(blocks, starts_ref, base):
    deep = blocks[0].shape[0] // 2
    pieces = []
    for b, block in enumerate(blocks[:3]):
        for part in range(2):
            pieces.append((block.at[part * deep : (part + 1) * deep, :], starts_ref[2 * b + part] - base))
    for b, block in enumerate(blocks[3:]):
        past = blocks[4].shape[0] if b == 2 else 0
        pieces.append((block, starts_ref[min(6 + b, 7)] + past - base))
    return pieces


def place(begin, pieces, full):
    for piece, start in pieces:
        begin(piece, full.at[pl.ds(pl.multiple_of(start, 16), piece.shape[0]), :])


def early_kernel(starts_ref, bases_ref, near, near_c, b0, b1, b2, sums_ref, x_rows, full, sem):
    half = x_rows.shape[2]
    copies, begin = starter(sem)
    begin(near.at[:, :half, :], x_rows.at[0])
    begin(near_c.at[:, :half, :], x_rows.at[1])
    place(begin, pieces_of((b0, b1, b2), starts_ref, 0), full)
    for copy in copies:
        copy.wait()
    total, chunk = sums_ref.shape[0], b0.shape[0]
    x_all = x_rows.reshape(total, full.shape[0])
    for m in range(total // TILE):
        at = slice(m * TILE, (m + 1) * TILE)
        sums = None
        for b in range(3):
            here = pl.ds(pl.multiple_of(bases_ref[b], 128), chunk)
            part = jnp.dot(x_all[at, here], full[here, :], preferred_element_type=jnp.float32)
            sums = part if sums is None else sums + part
        sums_ref[at, :] = sums


def hidden_kernel(starts_ref, bases_ref, near, near_c, b3, b4, b5, sums_hbm, hidden_ref, x_rows, full, sums, sem):
    half, chunk = x_rows.shape[2], x_rows.shape[3]
    copies, begin = starter(sem)
    base = pl.multiple_of(bases_ref[3], 128)
    begin(near.at[:, :half, pl.ds(base, chunk)], x_rows.at[0])
    begin(near_c.at[:, :half, pl.ds(base, chunk)], x_rows.at[1])
    place(begin, [(b3, starts_ref[6] - base), (b4, starts_ref[7] - base), (b5, starts_ref[7] - base + b4.shape[0])], full)
    begin(sums_hbm, sums)
    for copy in copies:
        copy.wait()
    total, units = hidden_ref.shape
    x_all = x_rows.reshape(total, chunk)
    for m in range(total // TILE):
        at = slice(m * TILE, (m + 1) * TILE)
        both = sums[at, :] + jnp.dot(x_all[at, :], full[...], preferred_element_type=jnp.float32)
        hidden_ref[at, :] = (jax.nn.silu(both[:, :units]) * both[:, units:]).astype(jnp.bfloat16)


def last_kernel(starts_ref, line_ref, far, far_c, near, near_c, b0, b1, b2, b3, b4, b5, hidden_near, *refs):
    outs = refs[:4]
    x_rows, y_far, y_near, full, hidden_far, done, sem, out_sem = refs[4:]
    half, n_half = x_rows.shape[2], y_near.shape[2]
    copies, begin = starter(sem)
    place(begin, pieces_of((b0, b1, b2, b3, b4, b5), starts_ref, 0), full)
    for core, rows in enumerate((far, far_c)):
        begin(rows.at[:, :half, :], x_rows.at[core])
    for core, rows in enumerate((near, near_c)):
        begin(rows.at[:, n_half:, :], y_near.at[core])
    for core, rows in enumerate((far, far_c)):
        begin(rows.at[:, half:, :], y_far.at[core])
    for copy in copies[:-4]:
        copy.wait()
    gate_rows(x_rows, full, hidden_far)
    for copy in copies[-4:]:
        copy.wait()
    width = full.shape[0]
    y_n, y_f = y_near.reshape(hidden_near.shape[0], width), y_far.reshape(hidden_far.shape[0], width)
    deep = outs[0].shape[0]
    sent = []
    for d in range(width // WIDE):
        cols = slice(d * WIDE, (d + 1) * WIDE)
        done[:, cols] = (over_rows(hidden_near, y_n, cols) + over_rows(hidden_far, y_f, cols)).astype(jnp.bfloat16)
        for s in range(4):
            at = pl.multiple_of(lax.rem(line_ref[0] + s, 4) * deep, 16)
            sent.append(
                pltpu.make_async_copy(done.at[pl.ds(at, deep), cols], outs[s].at[:, cols], out_sem.at[len(sent)])
            )
            sent[-1].start()
    for copy in sent:
        copy.wait()


def call(body, smems, hbms, vmems, outs, scratch, flops, moved, to_hbm=False):
    smem, vmem = pl.BlockSpec(memory_space=pltpu.SMEM), pl.BlockSpec(memory_space=pltpu.VMEM)
    hbm = pl.BlockSpec(memory_space=pltpu.HBM)
    return pl.pallas_call(
        body,
        in_specs=[smem] * len(smems) + [hbm] * len(hbms) + [vmem] * len(vmems),
        out_specs=[hbm if to_hbm else vmem] * len(outs),
        out_shape=outs,
        scratch_shapes=scratch,
        compiler_params=pltpu.CompilerParams(vmem_limit_bytes=60 << 20),
        cost_estimate=pl.CostEstimate(flops=flops, bytes_accessed=moved, transcendentals=0),
    )(*smems, *hbms, *vmems)


def rows_of(half, width):
    return pltpu.VMEM((2, 16, half, width), jnp.bfloat16)


def early_sums(starts, bases, near, near_c, blocks):
    half, width, both = near.shape[1] // 2, near.shape[2], blocks[0].shape[1]
    rows = 32 * half
    return call(
        early_kernel, (starts, bases), (near, near_c, *blocks[:3]), (),
        [jax.ShapeDtypeStruct((rows, both), jnp.float32)],
        [rows_of(half, width), pltpu.VMEM((width, both), jnp.bfloat16), pltpu.SemaphoreType.DMA((8,))],
        rows * both * width * 3 // 2, 2 * rows * width + 2 * width * both + 4 * rows * both,
    )[0]


def hidden_near(starts, bases, near, near_c, blocks, sums):
    half, chunk, both = near.shape[1] // 2, blocks[0].shape[0], blocks[0].shape[1]
    rows = 32 * half
    return call(
        hidden_kernel, (starts, bases), (near, near_c, *blocks[3:], sums), (),
        [jax.ShapeDtypeStruct((rows, both // 2), jnp.bfloat16)],
        [
            rows_of(half, chunk), pltpu.VMEM((chunk, both), jnp.bfloat16), pltpu.VMEM((rows, both), jnp.float32),
            pltpu.SemaphoreType.DMA((6,)),
        ],
        2 * rows * both * chunk, 2 * (rows + both) * chunk + 5 * rows * both,
    )[0]


def chunks(starts, line, far, far_c, near, near_c, blocks, hidden):
    f_half, n_half, width = far.shape[1] // 2, near.shape[1] // 2, far.shape[2]
    units, rows = hidden.shape[1], 32 * (f_half + n_half)
    return call(
        last_kernel, (starts, line), (far, far_c, near, near_c, *blocks), (hidden,),
        [jax.ShapeDtypeStruct((units // 4, width), jnp.bfloat16)] * 4,
        [
            rows_of(f_half, width), rows_of(f_half, width), rows_of(n_half, width),
            pltpu.VMEM((width, 2 * units), jnp.bfloat16), pltpu.VMEM((32 * f_half, units), jnp.bfloat16),
            pltpu.VMEM((units, width), jnp.bfloat16), pltpu.SemaphoreType.DMA((15,)), pltpu.SemaphoreType.DMA((20,)),
        ],
        2 * rows * units * width + 128 * f_half * units * width, 6 * width * units + rows * width * 2, True,
    )


def pack_kernel(flag_ref, core_ref, gate_ref, up_ref, other_gate_ref, other_up_ref, mine_ref, theirs_ref):
    swapped = flag_ref[0] == 1
    units = gate_ref.shape[1]
    unit = lax.broadcasted_iota(jnp.int32, (units, units // 2), 0)
    column = lax.broadcasted_iota(jnp.int32, (units, units // 2), 1)
    for target, core in ((mine_ref, core_ref[0]), (theirs_ref, 1 - core_ref[0])):
        chosen = (unit == (column // 96 * 2 + core) * 96 + column % 96).astype(jnp.bfloat16)
        for at, here, there in ((0, gate_ref, other_gate_ref), (1, up_ref, other_up_ref)):
            held = jnp.where(swapped, there[...], here[...])
            target[:, at * units // 2 : (at + 1) * units // 2] = jnp.dot(
                held, chosen, preferred_element_type=jnp.float32
            ).astype(jnp.bfloat16)


def pack(flag, core, *matrices):
    smem, vmem = pl.BlockSpec(memory_space=pltpu.SMEM), pl.BlockSpec(memory_space=pltpu.VMEM)
    shape = jax.ShapeDtypeStruct(matrices[0].shape, jnp.bfloat16)
    return pl.pallas_call(
        pack_kernel, in_specs=[smem] * 2 + [vmem] * 4, out_specs=[vmem] * 2, out_shape=[shape] * 2
    )(flag, core, *matrices)


def together(*values):
    return lax.optimization_barrier(values)


def z_steps(step_of):
    pairs = []
    for line in range(4):
        to, by = step_of[line]
        pairs += [(line * 4 + hi, to * 4 + (hi + by) % 4) for hi in range(4)]
    return pairs


def shards(tokens, cotangent, w_gate, w_up, expert_ids, gate_num, swap_flags):
    tok_count, width = tokens.shape
    deep = w_gate.shape[1]
    ahead, back = [(i, (i + 1) % 4) for i in range(4)], [(i, (i - 1) % 4) for i in range(4)]
    opposite = [(i, (i + 2) % 4) for i in range(4)]
    cores = [(0, 1), (1, 0)]
    along_z = ("zl", "zh")
    first = z_steps([(0, 1), (2, -1), (1, 1), (3, -1)])
    second = z_steps([(2, -1), (0, 1), (3, -1), (1, 1)])
    onward = z_steps([(0, 1), (1, 1), (2, -1), (3, -1)])
    place, line, core = lax.axis_index("zh"), lax.axis_index("zl"), lax.axis_index("c")
    me = (lax.axis_index("x") * 4 + place) * 4 + lax.axis_index("y")
    select = functools.partial(route, swap_flags, place.reshape(1), width)
    meta = jnp.concatenate([expert_ids, gate_num], axis=1).astype(jnp.bfloat16)
    meta = jnp.pad(meta, ((0, tok_count), (0, 128 - meta.shape[1])))
    own = jnp.concatenate([jnp.concatenate([tokens, cotangent], axis=0), meta], axis=1)
    rows_a, rows_b = lax.ppermute(own, along_z, first), lax.ppermute(own, along_z, second)
    flag = lax.dynamic_slice(swap_flags, (me % 32,), (1,))
    mine, theirs = pack(
        flag,
        core.reshape(1),
        w_gate[0],
        w_up[0],
        lax.ppermute(w_gate[0], "x", opposite),
        lax.ppermute(w_up[0], "x", opposite),
    )
    block = jnp.concatenate([mine, lax.ppermute(theirs, "c", cores)], axis=0)
    near_send, rows_a = together(select([(own, own), (rows_a, rows_a), (rows_b, rows_b)]), rows_a)
    rows_f = lax.ppermute(rows_a, along_z, onward)
    block_l, block_r = lax.ppermute(block, "zl", ahead), lax.ppermute(block, "zl", back)
    early = deep + deep // 4
    near, far_send, block_l, block_r, block_fl, block_fr = together(
        lax.all_to_all(near_send, PLANE, 0, 0, tiled=True),
        select([(rows_f, rows_f)]),
        block_l,
        block_r,
        lax.ppermute(block_l[:deep], "zl", ahead),
        lax.ppermute(block_r[deep:early], "zl", back),
    )
    rest_fr = lax.ppermute(block_r[early:], "zl", back)
    far = lax.all_to_all(far_send, PLANE, 0, 0, tiled=True)
    near_c = lax.ppermute(near, "c", cores)
    away = jnp.array([0, 0, 3, 3, 1, 1, 2, 2], jnp.int32)
    which = jnp.array([0, 1, 0, 1, 0, 1, 0, 1], jnp.int32)
    starts = (2 * ((line + away) % 4) + (core + which) % 2) * deep
    bases = (line + jnp.array([0, 3, 1, 2], jnp.int32)) % 4 * (2 * deep)
    blocks = [block, block_l, block_r, block_fl, block_fr, rest_fr]
    sums = early_sums(starts, bases, near, near_c, blocks)
    hidden = hidden_near(starts, bases, near, near_c, blocks, sums)
    far, hidden = together(far, hidden)
    far_c = lax.ppermute(far, "c", cores)
    parts = chunks(starts, line.reshape(1), far, far_c, near, near_c, blocks, hidden)
    total = parts[0].astype(jnp.float32)
    for s in (2, 1, 3):
        total += lax.ppermute(parts[s], "zl", [(i, (i + s) % 4) for i in range(4)]).astype(jnp.float32)
    return total[None]


def solution(mesh):
    fine = Mesh(mesh.devices.reshape(4, 2, 4, 4, 4), ("zl", "c", "x", "zh", "y"))
    rows = P(("zl", "c", "x", "zh", "y"), None)
    split = P(("x", "zh", "y"), ("zl", "c"), None)
    in_specs = (rows, rows, split, split, rows, rows, P())
    return jax.shard_map(shards, mesh=fine, in_specs=in_specs, out_specs=split, check_vma=False)
```

```python
import functools

import jax
import jax.numpy as jnp
from jax import lax
from jax.experimental import pallas as pl
from jax.experimental.pallas import tpu as pltpu
from jax.sharding import Mesh, PartitionSpec as P

PLANE = ("x", "y")
RANKS = 8


def route_kernel(count, flags_ref, place_ref, *refs):
    metas, xs, ys = refs[:count], refs[count : 2 * count], refs[2 * count : 3 * count]
    out_ref, pick_ref, weigh_ref = refs[3 * count :]
    tok_count = metas[0].shape[0]
    slots = pick_ref.shape[2]

    @pl.when(pl.program_id(0) == 0)
    def _():
        lane = lax.broadcasted_iota(jnp.int32, (1, slots), 1)
        expert = jnp.zeros((1, slots), jnp.int32)
        for j in range(16):
            home = (j // 4) * 16 + place_ref[0] * 4 + j % 4
            other = lax.rem(home + 32, 64)
            held = jnp.where(flags_ref[lax.rem(home, 32)] == 1, other, home)
            expert = jnp.where(lane // RANKS == j, held, expert)
        expert = expert.astype(jnp.float32)
        rank_of = (lane % RANKS).astype(jnp.float32)
        earlier = (
            lax.broadcasted_iota(jnp.int32, (tok_count, tok_count), 0)
            > lax.broadcasted_iota(jnp.int32, (tok_count, tok_count), 1)
        ).astype(jnp.bfloat16)
        for s in range(count):
            meta = metas[s][...].astype(jnp.float32)
            weight = jnp.zeros((tok_count, slots), jnp.float32)
            for k in range(6):
                weight = jnp.where(meta[:, k : k + 1] == expert, meta[:, 6 + k : 7 + k], weight)
            chosen = jnp.where(weight > 0.0, 1.0, 0.0)
            before = jnp.dot(earlier, chosen.astype(jnp.bfloat16), preferred_element_type=jnp.float32)
            here = before == rank_of
            pick_ref[s] = jnp.where(here, chosen, 0.0).astype(jnp.bfloat16)
            weigh_ref[s] = jnp.where(here, weight * (1.0 / 64.0), 0.0).astype(jnp.bfloat16)

    for base, picks, rows in ((0, pick_ref, xs), (count, weigh_ref, ys)):
        for s in range(count):
            picked = lax.dot_general(
                picks[s], rows[s][...], (((0,), (0,)), ((), ())), preferred_element_type=jnp.float32
            )
            at = (base + s) * RANKS
            out_ref[:, at : at + RANKS, :] = picked.reshape(16, RANKS, picked.shape[1]).astype(jnp.bfloat16)


def route(flags, place, width, sources):
    count = len(sources)
    tok_count = 64
    tile = 512
    meta_block = width // 128
    smem = pl.BlockSpec(memory_space=pltpu.SMEM)
    x_of, y_of = [pair[0] for pair in sources], [pair[1] for pair in sources]
    y_block = 1 if x_of[0] is y_of[0] else 0
    return pl.pallas_call(
        functools.partial(route_kernel, count),
        grid=(width // tile,),
        in_specs=[smem] * 2
        + [pl.BlockSpec((tok_count, 128), lambda i: (0, meta_block))] * count
        + [pl.BlockSpec((tok_count, tile), lambda i: (0, i))] * count
        + [pl.BlockSpec((tok_count, tile), lambda i: (y_block, i))] * count,
        out_specs=pl.BlockSpec((16, 2 * count * RANKS, tile), lambda i: (0, 0, i)),
        out_shape=jax.ShapeDtypeStruct((16, 2 * count * RANKS, width), jnp.bfloat16),
        scratch_shapes=[pltpu.VMEM((count, tok_count, 16 * RANKS), jnp.bfloat16)] * 2,
        cost_estimate=pl.CostEstimate(
            flops=40_000_000_000,
            bytes_accessed=2 * count * (tok_count + 128) * width * 2,
            transcendentals=0,
        ),
    )(flags, place, *x_of, *x_of, *y_of)


def gate_rows(x_rows, full, hidden):
    total, units = hidden.shape
    x_all = x_rows.reshape(total, full.shape[0])
    tile = 256
    for m in range(total // tile):
        at = slice(m * tile, (m + 1) * tile)
        sums = jnp.dot(x_all[at, :], full[...], preferred_element_type=jnp.float32)
        hidden[at, :] = (jax.nn.silu(sums[:, :units]) * sums[:, units:]).astype(jnp.bfloat16)


def over_rows(hidden, y_rows, cols):
    return lax.dot_general(
        hidden[...], y_rows[:, cols], (((0,), (0,)), ((), ())), preferred_element_type=jnp.float32
    )


def starter(sem):
    copies = []

    def begin(source, target):
        copies.append(pltpu.make_async_copy(source, target, sem.at[len(copies)]))
        copies[-1].start()

    return copies, begin


WIDE = 512
TILE = 256


def pieces_of(blocks, starts_ref, base):
    deep = blocks[0].shape[0] // 2
    pieces = []
    for b, block in enumerate(blocks[:3]):
        for part in range(2):
            pieces.append((block.at[part * deep : (part + 1) * deep, :], starts_ref[2 * b + part] - base))
    for b, block in enumerate(blocks[3:]):
        past = blocks[4].shape[0] if b == 2 else 0
        pieces.append((block, starts_ref[min(6 + b, 7)] + past - base))
    return pieces


def place(begin, pieces, full):
    for piece, start in pieces:
        begin(piece, full.at[pl.ds(pl.multiple_of(start, 16), piece.shape[0]), :])


def early_kernel(starts_ref, bases_ref, near, near_c, b0, b1, b2, sums_ref, x_rows, full, sem):
    half = x_rows.shape[2]
    copies, begin = starter(sem)
    begin(near.at[:, :half, :], x_rows.at[0])
    begin(near_c.at[:, :half, :], x_rows.at[1])
    place(begin, pieces_of((b0, b1, b2), starts_ref, 0), full)
    total, chunk = sums_ref.shape[0], b0.shape[0]
    x_all = x_rows.reshape(total, full.shape[0])
    for b in range(3):
        for copy in copies[2 * b + 2 if b else 0 : 2 * b + 4]:
            copy.wait()
        here = pl.ds(pl.multiple_of(bases_ref[b], 128), chunk)
        for m in range(total // TILE):
            at = slice(m * TILE, (m + 1) * TILE)
            part = jnp.dot(x_all[at, here], full[here, :], preferred_element_type=jnp.float32)
            sums_ref[at, :] = sums_ref[at, :] + part if b else part


def hidden_kernel(starts_ref, bases_ref, near, near_c, b3, b4, b5, sums_hbm, hidden_ref, x_rows, full, sums, sem):
    half, chunk = x_rows.shape[2], x_rows.shape[3]
    copies, begin = starter(sem)
    base = pl.multiple_of(bases_ref[3], 128)
    begin(near.at[:, :half, pl.ds(base, chunk)], x_rows.at[0])
    begin(near_c.at[:, :half, pl.ds(base, chunk)], x_rows.at[1])
    place(begin, [(b3, starts_ref[6] - base), (b4, starts_ref[7] - base), (b5, starts_ref[7] - base + b4.shape[0])], full)
    begin(sums_hbm, sums)
    for copy in copies:
        copy.wait()
    total, units = hidden_ref.shape
    x_all = x_rows.reshape(total, chunk)
    for m in range(total // TILE):
        at = slice(m * TILE, (m + 1) * TILE)
        both = sums[at, :] + jnp.dot(x_all[at, :], full[...], preferred_element_type=jnp.float32)
        hidden_ref[at, :] = (jax.nn.silu(both[:, :units]) * both[:, units:]).astype(jnp.bfloat16)


def last_kernel(starts_ref, line_ref, far, far_c, near, near_c, b0, b1, b2, b3, b4, b5, hidden_near, *refs):
    outs = refs[:4]
    x_rows, y_far, y_near, full, hidden_far, done, sem, out_sem = refs[4:]
    half, n_half = x_rows.shape[2], y_near.shape[2]
    copies, begin = starter(sem)
    place(begin, pieces_of((b0, b1, b2, b3, b4, b5), starts_ref, 0), full)
    for core, rows in enumerate((far, far_c)):
        begin(rows.at[:, :half, :], x_rows.at[core])
    for core, rows in enumerate((near, near_c)):
        begin(rows.at[:, n_half:, :], y_near.at[core])
    for core, rows in enumerate((far, far_c)):
        begin(rows.at[:, half:, :], y_far.at[core])
    for copy in copies[:-4]:
        copy.wait()
    gate_rows(x_rows, full, hidden_far)
    for copy in copies[-4:]:
        copy.wait()
    width = full.shape[0]
    y_n, y_f = y_near.reshape(hidden_near.shape[0], width), y_far.reshape(hidden_far.shape[0], width)
    deep = outs[0].shape[0]
    sent = []
    for d in range(width // WIDE):
        cols = slice(d * WIDE, (d + 1) * WIDE)
        done[:, cols] = (over_rows(hidden_near, y_n, cols) + over_rows(hidden_far, y_f, cols)).astype(jnp.bfloat16)
        for s in range(4):
            at = pl.multiple_of(lax.rem(line_ref[0] + s, 4) * deep, 16)
            sent.append(
                pltpu.make_async_copy(done.at[pl.ds(at, deep), cols], outs[s].at[:, cols], out_sem.at[len(sent)])
            )
            sent[-1].start()
    for copy in sent:
        copy.wait()


def call(body, smems, hbms, vmems, outs, scratch, flops, moved, to_hbm=False):
    smem, vmem = pl.BlockSpec(memory_space=pltpu.SMEM), pl.BlockSpec(memory_space=pltpu.VMEM)
    hbm = pl.BlockSpec(memory_space=pltpu.HBM)
    return pl.pallas_call(
        body,
        in_specs=[smem] * len(smems) + [hbm] * len(hbms) + [vmem] * len(vmems),
        out_specs=[hbm if to_hbm else vmem] * len(outs),
        out_shape=outs,
        scratch_shapes=scratch,
        compiler_params=pltpu.CompilerParams(vmem_limit_bytes=60 << 20),
        cost_estimate=pl.CostEstimate(flops=flops, bytes_accessed=moved, transcendentals=0),
    )(*smems, *hbms, *vmems)


def rows_of(half, width):
    return pltpu.VMEM((2, 16, half, width), jnp.bfloat16)


def early_sums(starts, bases, near, near_c, blocks):
    half, width, both = near.shape[1] // 2, near.shape[2], blocks[0].shape[1]
    rows = 32 * half
    return call(
        early_kernel, (starts, bases), (near, near_c, *blocks[:3]), (),
        [jax.ShapeDtypeStruct((rows, both), jnp.float32)],
        [rows_of(half, width), pltpu.VMEM((width, both), jnp.bfloat16), pltpu.SemaphoreType.DMA((8,))],
        rows * both * width * 3 // 2, 2 * rows * width + 2 * width * both + 4 * rows * both,
    )[0]


def hidden_near(starts, bases, near, near_c, blocks, sums):
    half, chunk, both = near.shape[1] // 2, blocks[0].shape[0], blocks[0].shape[1]
    rows = 32 * half
    return call(
        hidden_kernel, (starts, bases), (near, near_c, *blocks[3:], sums), (),
        [jax.ShapeDtypeStruct((rows, both // 2), jnp.bfloat16)],
        [
            rows_of(half, chunk), pltpu.VMEM((chunk, both), jnp.bfloat16), pltpu.VMEM((rows, both), jnp.float32),
            pltpu.SemaphoreType.DMA((6,)),
        ],
        2 * rows * both * chunk, 2 * (rows + both) * chunk + 5 * rows * both,
    )[0]


def chunks(starts, line, far, far_c, near, near_c, blocks, hidden):
    f_half, n_half, width = far.shape[1] // 2, near.shape[1] // 2, far.shape[2]
    units, rows = hidden.shape[1], 32 * (f_half + n_half)
    return call(
        last_kernel, (starts, line), (far, far_c, near, near_c, *blocks), (hidden,),
        [jax.ShapeDtypeStruct((units // 4, width), jnp.bfloat16)] * 4,
        [
            rows_of(f_half, width), rows_of(f_half, width), rows_of(n_half, width),
            pltpu.VMEM((width, 2 * units), jnp.bfloat16), pltpu.VMEM((32 * f_half, units), jnp.bfloat16),
            pltpu.VMEM((units, width), jnp.bfloat16), pltpu.SemaphoreType.DMA((15,)), pltpu.SemaphoreType.DMA((20,)),
        ],
        2 * rows * units * width + 128 * f_half * units * width, 6 * width * units + rows * width * 2, True,
    )


def pack_kernel(flag_ref, core_ref, gate_ref, up_ref, other_gate_ref, other_up_ref, mine_ref, theirs_ref):
    swapped = flag_ref[0] == 1
    units = gate_ref.shape[1]
    unit = lax.broadcasted_iota(jnp.int32, (units, units // 2), 0)
    column = lax.broadcasted_iota(jnp.int32, (units, units // 2), 1)
    for target, core in ((mine_ref, core_ref[0]), (theirs_ref, 1 - core_ref[0])):
        chosen = (unit == (column // 96 * 2 + core) * 96 + column % 96).astype(jnp.bfloat16)
        for at, here, there in ((0, gate_ref, other_gate_ref), (1, up_ref, other_up_ref)):
            held = jnp.where(swapped, there[...], here[...])
            target[:, at * units // 2 : (at + 1) * units // 2] = jnp.dot(
                held, chosen, preferred_element_type=jnp.float32
            ).astype(jnp.bfloat16)


def pack(flag, core, *matrices):
    smem, vmem = pl.BlockSpec(memory_space=pltpu.SMEM), pl.BlockSpec(memory_space=pltpu.VMEM)
    shape = jax.ShapeDtypeStruct(matrices[0].shape, jnp.bfloat16)
    return pl.pallas_call(
        pack_kernel, in_specs=[smem] * 2 + [vmem] * 4, out_specs=[vmem] * 2, out_shape=[shape] * 2
    )(flag, core, *matrices)


def together(*values):
    return lax.optimization_barrier(values)


def z_steps(step_of):
    pairs = []
    for line in range(4):
        to, by = step_of[line]
        pairs += [(line * 4 + hi, to * 4 + (hi + by) % 4) for hi in range(4)]
    return pairs


def shards(tokens, cotangent, w_gate, w_up, expert_ids, gate_num, swap_flags):
    tok_count, width = tokens.shape
    deep = w_gate.shape[1]
    ahead, back = [(i, (i + 1) % 4) for i in range(4)], [(i, (i - 1) % 4) for i in range(4)]
    opposite = [(i, (i + 2) % 4) for i in range(4)]
    cores = [(0, 1), (1, 0)]
    along_z = ("zl", "zh")
    first = z_steps([(0, 1), (2, -1), (1, 1), (3, -1)])
    second = z_steps([(2, -1), (0, 1), (3, -1), (1, 1)])
    onward = z_steps([(0, 1), (1, 1), (2, -1), (3, -1)])
    place, line, core = lax.axis_index("zh"), lax.axis_index("zl"), lax.axis_index("c")
    me = (lax.axis_index("x") * 4 + place) * 4 + lax.axis_index("y")
    select = functools.partial(route, swap_flags, place.reshape(1), width)
    meta = jnp.concatenate([expert_ids, gate_num], axis=1).astype(jnp.bfloat16)
    meta = jnp.pad(meta, ((0, tok_count), (0, 128 - meta.shape[1])))
    own = jnp.concatenate([jnp.concatenate([tokens, cotangent], axis=0), meta], axis=1)
    rows_a, rows_b = lax.ppermute(own, along_z, first), lax.ppermute(own, along_z, second)
    flag = lax.dynamic_slice(swap_flags, (me % 32,), (1,))
    mine, theirs = pack(
        flag,
        core.reshape(1),
        w_gate[0],
        w_up[0],
        lax.ppermute(w_gate[0], "x", opposite),
        lax.ppermute(w_up[0], "x", opposite),
    )
    block = jnp.concatenate([mine, lax.ppermute(theirs, "c", cores)], axis=0)
    near_send, rows_a = together(select([(own, own), (rows_a, rows_a), (rows_b, rows_b)]), rows_a)
    rows_f = lax.ppermute(rows_a, along_z, onward)
    block_l, block_r = lax.ppermute(block, "zl", ahead), lax.ppermute(block, "zl", back)
    early = deep + deep // 4
    near, far_send, block_l, block_r, block_fl, block_fr = together(
        lax.all_to_all(near_send, PLANE, 0, 0, tiled=True),
        select([(rows_f, rows_f)]),
        block_l,
        block_r,
        lax.ppermute(block_l[:deep], "zl", ahead),
        lax.ppermute(block_r[deep:early], "zl", back),
    )
    rest_fr = lax.ppermute(block_r[early:], "zl", back)
    far = lax.all_to_all(far_send, PLANE, 0, 0, tiled=True)
    near_c = lax.ppermute(near, "c", cores)
    away = jnp.array([0, 0, 3, 3, 1, 1, 2, 2], jnp.int32)
    which = jnp.array([0, 1, 0, 1, 0, 1, 0, 1], jnp.int32)
    starts = (2 * ((line + away) % 4) + (core + which) % 2) * deep
    bases = (line + jnp.array([0, 3, 1, 2], jnp.int32)) % 4 * (2 * deep)
    blocks = [block, block_l, block_r, block_fl, block_fr, rest_fr]
    sums = early_sums(starts, bases, near, near_c, blocks)
    hidden = hidden_near(starts, bases, near, near_c, blocks, sums)
    far, hidden = together(far, hidden)
    far_c = lax.ppermute(far, "c", cores)
    parts = chunks(starts, line.reshape(1), far, far_c, near, near_c, blocks, hidden)
    total = parts[0].astype(jnp.float32)
    for s in (2, 1, 3):
        total += lax.ppermute(parts[s], "zl", [(i, (i + s) % 4) for i in range(4)]).astype(jnp.float32)
    return total[None]


def solution(mesh):
    fine = Mesh(mesh.devices.reshape(4, 2, 4, 4, 4), ("zl", "c", "x", "zh", "y"))
    rows = P(("zl", "c", "x", "zh", "y"), None)
    split = P(("x", "zh", "y"), ("zl", "c"), None)
    in_specs = (rows, rows, split, split, rows, rows, P())
    return jax.shard_map(shards, mesh=fine, in_specs=in_specs, out_specs=split, check_vma=False)
```
